512 devices in a mesh: lat: 32 (over x_hi, y, core), lon: 16 (over x_lo, z).
Axes of the slice: x: 4 (x_hi: 2, x_lo: 2; x = x_hi * 2 + x_lo), y: 8, z: 8, core: 2. Of those that a mesh axis runs over, the one named last changes fastest.
Arguments:
- air_condition_inputs: bfloat16 [48, 128, 1440], P(None, 'lat'), may hold values from -6 to 6
- air_embedding_matrix: bfloat16 [48, 512], P(None, 'lon'), may hold values from -0.875 to 0.875
- air_blending_matrix: bfloat16 [512, 512], P(None, 'lon'), may hold values from -0.25 to 0.25
- exchange_readout_matrix: bfloat16 [512, 8], P('lon'), may hold values from -0.25 to 0.25
- overlay_share_factors: bfloat16 [128, 1440, 2048], P('lat', 'lon'), may hold values from 0 to 2, as said below
- marine_condition_inputs: bfloat16 [76, 512, 2048], P(None, 'lat', 'lon'), may hold values from -6 to 6
- water_embedding_matrix: bfloat16 [76, 256], replicated, may hold values from -0.625 to 0.625
- drive_lifting_matrix: bfloat16 [8, 256], replicated, may hold values from -6 to 6
- segment_stencil_factors: bfloat16 [2, 3, 3, 256, 256], replicated, may hold values from -0.125 to 0.125
- thermal_readout_matrix: bfloat16 [256], replicated, may hold values from -0.375 to 0.375
- water_point_indicator: int32 [512, 2048], P('lat', 'lon'), may hold values 0 or 1
Outputs:
- surface_temp: float32 [512, 2048], P('lat', 'lon')
The draws below stay inside these ranges and needn't reach their ends.
Inputs may be any that keep to these rules, and one draw needn't show every extreme that they name: `water_point_indicator`: 1 marks an ocean cell, 0 a land cell. `overlay_share_factors`: an entry is nonzero only where the atmosphere cell and the ocean cell intersect in latitude and longitude (1 to 4 atmosphere cells for each ocean cell); most entries are zero. The weights of one ocean cell sum to at least 0.5.
All inputs are finite; a program needn't handle non-finite values. No bound on the sum of `water_point_indicator` on one device may be relied on, other than what follows from the above.
Results may differ from the reference program's by a relative error of at most 0.0063.
Values may be sent and summed in bfloat16 or wider, within the bound.
No kernel may reach another device: no remote copies, remote signals or barrier semaphores. Data moves between devices by JAX's collectives and lax.ppermute only.
A program may use at most 64 MiB of HBM per device.

```python
import jax
import jax.numpy as jnp
from jax import lax

AFIELDS = 48
WA = 512
OFIELDS = 76
SEA_FEATURE_COUNT = 256
FL = 8
SECTIONS = 2
ALON = 1440
AR = 4
OY = 16
OX = 128
NAY = 128
NYO = 512
NXO = 2048
N_LAT = 32
N_LON = 16


def draw_overlay_share_factors(key, part):
    lon_width = ALON // N_LON
    row_unit = AR / OY
    col_unit = lon_width / OX
    atm_row = (jnp.arange(NAY, dtype=jnp.int32) % AR).astype(jnp.float32)[:, None, None]
    atm_col = (jnp.arange(ALON, dtype=jnp.int32) % lon_width).astype(jnp.float32)[None, :, None]
    cells = jnp.arange(OY * OX, dtype=jnp.int32)
    sea_row = (cells // OX).astype(jnp.float32)[None, None, :]
    sea_col = (cells % OX).astype(jnp.float32)[None, None, :]
    over_rows = jnp.maximum(jnp.minimum(atm_row + 1.0, (sea_row + 1.0) * row_unit) - jnp.maximum(atm_row, sea_row * row_unit), 0.0)
    over_cols = jnp.maximum(jnp.minimum(atm_col + 1.0, (sea_col + 1.0) * col_unit) - jnp.maximum(atm_col, sea_col * col_unit), 0.0)
    share = over_rows * over_cols / (row_unit * col_unit)
    factor = jnp.exp(jax.random.uniform(key, (NAY, ALON, OY * OX), jnp.float32, -0.6931472, 0.6931472))
    return (share * factor).astype(jnp.bfloat16)


def set_ends(drawn, stream_key, least, high):
    extent = drawn.shape
    place = [jax.random.randint(jax.random.fold_in(stream_key, axis), (), 0, extent[axis]) for axis in range(len(extent))]
    drawn = drawn.at[tuple(place)].set(least)
    longest = extent.index(max(extent))
    place[longest] = (place[longest] + 1) % extent[longest]
    return drawn.at[tuple(place)].set(high)


def block_levels(own_key, dims, shards, smallest, top_value):
    factor_of, own = 1.0, jax.random.fold_in(own_key, 6)
    for position, blocks in shards:
        heights = jnp.exp(jax.random.uniform(jax.random.fold_in(own, position), (blocks,), jnp.float32, smallest / len(shards), top_value / len(shards)))
        factor_of = factor_of * jnp.repeat(heights, dims[position] // blocks).reshape([-1 if axis == position else 1 for axis in range(len(dims))])
    return factor_of


def centred(key, shape, spread, bound, split=(), kind=jnp.bfloat16):
    values = jax.random.normal(key, shape, jnp.float32) * spread
    if len(split) > 0:
        values = block_levels(key, shape, split, -0.22, 0.18) * values
    return jnp.clip(values, min=-bound, max=bound).astype(kind)


def setup_inputs(seed: int = 0) -> dict:
    key_list = jax.random.split(jax.random.key(seed), 12)
    return {
        "air_condition_inputs": centred(key_list[0], (AFIELDS, NAY, ALON), 1.0, 6.0, ((1, 32),)),
        "air_embedding_matrix": centred(key_list[1], (AFIELDS, WA), AFIELDS ** -0.5, 0.875, ((1, 16),)),
        "air_blending_matrix": centred(key_list[2], (WA, WA), WA ** -0.5, 0.25, ((1, 16),)),
        "exchange_readout_matrix": centred(key_list[3], (WA, FL), WA ** -0.5, 0.25, ((0, 16),)),
        "overlay_share_factors": draw_overlay_share_factors(jax.random.fold_in(key_list[11], 71), 0),
        "marine_condition_inputs": centred(key_list[5], (OFIELDS, NYO, NXO), 1.0, 6.0, ((1, 32), (2, 16))),
        "water_embedding_matrix": centred(key_list[6], (OFIELDS, SEA_FEATURE_COUNT), OFIELDS ** -0.5, 0.625),
        "drive_lifting_matrix": centred(key_list[7], (FL, SEA_FEATURE_COUNT), 1 ** -0.5, 6.0),
        "segment_stencil_factors": centred(key_list[8], (SECTIONS, 3, 3, SEA_FEATURE_COUNT, SEA_FEATURE_COUNT), (9 * SEA_FEATURE_COUNT) ** -0.5, 0.125),
        "thermal_readout_matrix": centred(key_list[9], (SEA_FEATURE_COUNT,), SEA_FEATURE_COUNT ** -0.5, 0.375),
        "water_point_indicator": set_ends((jax.random.randint(key_list[10], (NYO, NXO), 0, 10) < 7).astype(jnp.int32), jax.random.fold_in(key_list[10], 1), 0, 1),
    }


def activate(values):
    return jax.nn.gelu(values, approximate=True)


def conv_section(marine_current_condition, kernels, sea_mask):
    wide = jnp.concatenate([marine_current_condition[:, -1:], marine_current_condition, marine_current_condition[:, :1]], 1)
    ghost_row = wide[-1][::-1]
    south_row = jnp.zeros((1, wide.shape[1], wide.shape[2]), wide.dtype)
    padded = jnp.concatenate([south_row, wide, ghost_row[None]], 0)
    kernels_wide = kernels.astype(jnp.float32)

    def band_conv(band_idx):
        region = lax.dynamic_slice_in_dim(padded, band_idx * OY, OY + 2, 0).astype(jnp.float32)
        running = jnp.zeros((OY, NXO, SEA_FEATURE_COUNT), jnp.float32)
        for row_off in range(3):
            for col_off in range(3):
                window = region[row_off:row_off + OY, col_off:col_off + NXO]
                running = running + jnp.einsum('yxc,cd->yxd', window, kernels_wide[row_off, col_off])
        return running

    conv_out = lax.map(band_conv, jnp.arange(N_LAT, dtype=jnp.int32)).reshape(NYO, NXO, SEA_FEATURE_COUNT)
    return (sea_mask * (marine_current_condition.astype(jnp.float32) + activate(conv_out))).astype(jnp.bfloat16)


def reference(air_condition_inputs, air_embedding_matrix, air_blending_matrix, exchange_readout_matrix, overlay_share_factors, marine_condition_inputs, water_embedding_matrix, drive_lifting_matrix, segment_stencil_factors, thermal_readout_matrix, water_point_indicator):
    first_act = activate(jnp.einsum('frl,fc->crl', air_condition_inputs.astype(jnp.float32), air_embedding_matrix.astype(jnp.float32))).astype(jnp.bfloat16)
    second_act = activate(jnp.einsum('crl,cd->drl', first_act.astype(jnp.float32), air_blending_matrix.astype(jnp.float32))).astype(jnp.bfloat16)
    flux_out = jnp.einsum('crl,cf->rlf', second_act.astype(jnp.float32), exchange_readout_matrix.astype(jnp.float32)).astype(jnp.bfloat16)
    lon_width = ALON // N_LON
    tiles_w = overlay_share_factors.reshape(N_LAT, AR, N_LON, lon_width, OY * OX)
    tiles_f = flux_out.reshape(N_LAT, AR, N_LON, lon_width, FL)

    def regrid_band(pair):
        weights_band, flux_band = pair
        weights_band = weights_band.astype(jnp.float32)
        weighted = jnp.einsum('ajbt,ajbf->jtf', weights_band, flux_band.astype(jnp.float32))
        coverage = jnp.sum(weights_band, axis=(0, 2))
        return (weighted / coverage[..., None]).astype(jnp.bfloat16)

    forcing = lax.map(regrid_band, (tiles_w, tiles_f))
    forcing = forcing.reshape(N_LAT, N_LON, OY, OX, FL).transpose(0, 2, 1, 3, 4).reshape(NYO, NXO, FL)
    sea_mask = water_point_indicator.astype(jnp.float32)[..., None]
    encoded = jnp.einsum('fyx,fc->yxc', marine_condition_inputs.astype(jnp.float32), water_embedding_matrix.astype(jnp.float32))
    encoded = encoded + jnp.einsum('yxf,fc->yxc', forcing.astype(jnp.float32), drive_lifting_matrix.astype(jnp.float32))
    marine_current_condition = (activate(encoded) * sea_mask).astype(jnp.bfloat16)
    for section_idx in range(SECTIONS):
        marine_current_condition = conv_section(marine_current_condition, segment_stencil_factors[section_idx], sea_mask)
    topmost_sheet = jnp.einsum('phc,c->ph', marine_current_condition.astype(jnp.float32), thermal_readout_matrix.astype(jnp.float32))
    return topmost_sheet * sea_mask[..., 0]
```

```python
import jax
import jax.numpy as jnp
from jax import lax
from jax.experimental import pallas as pl
from jax.experimental.pallas import tpu as pltpu
from jax.sharding import PartitionSpec as P

BF = jnp.bfloat16
F32 = jnp.float32
LANES = 128
PAD = 8
HALO = 2
MM = 80
TILE = 384


def activate(values):
    inner = 0.7978845608028654 * (values + 0.044715 * (values * values * values))
    return 0.5 * values * (1.0 + jnp.tanh(inner))


def dot(a, b, dims=((1,), (0,))):
    return lax.dot_general(a, b, (dims, ((), ())), preferred_element_type=F32)


NT = ((1,), (1,))
TN = ((0,), (0,))


def edge_kernel(ov_ref, mm_ref, east_ref, west_ref):
    bands, width, cells = ov_ref.shape
    rows = cells // LANES
    n = HALO * rows
    which = lax.broadcasted_iota(jnp.int32, (2 * n, cells), 0)
    lane = lax.broadcasted_iota(jnp.int32, (2 * n, cells), 1)
    side = which // n
    inside = which % n
    target = (inside // HALO) * LANES + inside % HALO + side * (LANES - HALO)
    pick = (lane == target).astype(F32).astype(BF)
    east_ref[...] = jnp.zeros_like(east_ref)
    west_ref[...] = jnp.zeros_like(west_ref)
    for r in range(bands):
        got = dot(pick, ov_ref[r], NT).astype(BF)
        west_ref[:, r * LANES : r * LANES + width] = got[:n]
        east_ref[:, r * LANES : r * LANES + width] = got[n:]
    got = dot(pick, mm_ref[...], NT).astype(BF)
    west_ref[:, bands * LANES : bands * LANES + MM] = got[:n]
    east_ref[:, bands * LANES : bands * LANES + MM] = got[n:]


def pack_kernel(where_ref, ov_ref, mm_ref, rw_ref, re_ref, air_ref, a_ref, b_ref):
    bands, width, cells = ov_ref.shape

    def write(dst, top):
        first = cells - HALO * LANES if top else 0
        half = rw_ref.shape[0] // 2
        edge = half if top else 0
        for r in range(bands):
            for h in range(HALO):
                lanes = slice(first + h * LANES, first + (h + 1) * LANES)
                at = (r * HALO + h) * 96
                dst[at : at + width, :] = ov_ref[r, :, lanes]
        at = bands * HALO * 96
        for h in range(HALO):
            lanes = slice(first + h * LANES, first + (h + 1) * LANES)
            dst[at : at + MM, :] = mm_ref[:, lanes]
            at += MM
        for q in range(bands + 1):
            lanes = slice(q * LANES, (q + 1) * LANES)
            dst[at : at + half, :] = rw_ref[edge : edge + half, lanes]
            dst[at + half : at + 2 * half, :] = re_ref[edge : edge + half, lanes]
            at += 2 * half
        for q in range(air_ref.shape[1] // LANES):
            dst[at : at + 48, :] = air_ref[:, q * LANES : (q + 1) * LANES]
            at += 48

    even = where_ref[0] == 0

    @pl.when(even)
    def _():
        write(a_ref, True)
        write(b_ref, False)

    @pl.when(jnp.logical_not(even))
    def _():
        write(a_ref, False)
        write(b_ref, True)


def main_kernel(
    where_ref, wts_ref, air_ref, pa_ref, pb_ref, rw_ref, re_ref, ov_ref, mm_ref, sea_ref,
    wenc_ref, kw_ref, thermal_ref, out_ref,
    airs, flux, z, side, shifted, shifted2, mask,
):
    bands, width, cells = ov_ref.shape
    rows = cells // LANES
    c = kw_ref.shape[2]
    n = HALO * rows
    half = n // 2
    wide = LANES + 2 * PAD
    ext = rows + 2 * HALO
    even = where_ref[0] == 0
    north = where_ref[1] == 1
    chan = wts_ref.shape[0]
    at_mm = bands * HALO * 96
    at_edge = at_mm + HALO * MM
    at_air = at_edge + (bands + 1) * 2 * half

    def halo(which, lo, size):
        a, b = pa_ref[lo : lo + size, :], pb_ref[lo : lo + size, :]
        return jnp.where(even, a, b) if which == 0 else jnp.where(even, b, a)

    for k in range(3):
        airs[k] = air_ref[:, k * TILE : (k + 1) * TILE]
        for which in range(2):
            for q in range(TILE // LANES):
                airs[3 + 3 * which + k, :, q * LANES : (q + 1) * LANES] = halo(
                    which, at_air + (k * (TILE // LANES) + q) * 48, 48
                )

    def air_tile(k, _):
        first = activate(dot(wts_ref[:, chan : chan + 48], airs[k])).astype(BF)
        second = activate(dot(wts_ref[:, :chan], first)).astype(BF)
        got = dot(wts_ref[:, chan : chan + LANES], second, TN)[48:56].astype(BF).astype(F32)
        for r in range(bands):
            moved = got if r == 0 else pltpu.roll(got, TILE - r * width, 1)
            both = jnp.concatenate([moved[:, :LANES], jnp.ones((8, LANES), F32)], 0)
            flux[k, :, r * LANES : (r + 1) * LANES] = both.astype(BF)
        return 0

    lax.fori_loop(0, 9, air_tile, 0)

    def forced(sums):
        return sums[:8] / jnp.maximum(sums[8:], 0.25)

    sums = dot(flux[1, :, :width], ov_ref[0])
    for r in range(1, bands):
        sums = sums + dot(flux[1, :, r * LANES : r * LANES + width], ov_ref[r])
    z[:MM, :cells] = mm_ref[...]
    z[MM:, :cells] = jnp.concatenate([forced(sums), jnp.zeros((8, cells), F32)], 0).astype(BF)
    for which in range(2):
        for h in range(HALO):
            sums = None
            for r in range(bands):
                term = dot(
                    flux[3 + 3 * which + 1, :, r * LANES : r * LANES + width],
                    halo(which, (r * HALO + h) * 96, width),
                )
                sums = term if sums is None else sums + term
            lanes = slice(cells + (which * HALO + h) * LANES, cells + (which * HALO + h + 1) * LANES)
            z[:MM, lanes] = halo(which, at_mm + h * MM, MM)
            z[MM:, lanes] = jnp.concatenate([forced(sums), jnp.zeros((8, LANES), F32)], 0).astype(BF)

    def edge_cells(table, fields, k):
        flu = flux[k]
        weighted, coverage = dot(table, flu[:8], NT), dot(table, flu[8:], NT)
        forcing = (weighted / jnp.maximum(coverage, 0.25)).astype(BF)
        enc = dot(fields, jnp.concatenate([wenc_ref[:MM], jnp.zeros((LANES - MM, wenc_ref.shape[1]), BF)], 0))
        state = enc[:, :c] + dot(forcing, wenc_ref[MM : MM + 8, :c])
        m = enc[:, c:]
        state = activate(state) * jnp.concatenate([m, m], 1)
        return jnp.concatenate([state.astype(BF), m.astype(BF)], 1)

    for s in range(2):
        ref = (rw_ref, re_ref)[s]
        own = edge_cells(ref[:, : bands * LANES], ref[:, bands * LANES :], 2 * s)
        near = []
        for which in range(2):
            parts = [halo(which, at_edge + q * 2 * half + s * half, half) for q in range(bands + 1)]
            near.append(edge_cells(jnp.concatenate(parts[:-1], 1), parts[-1], 3 + 3 * which + 2 * s))
        table = jnp.concatenate([near[1], own, near[0]], 0)
        total = 2 * half + n
        at = lax.broadcasted_iota(jnp.int32, (ext * PAD, total), 0)
        lane = lax.broadcasted_iota(jnp.int32, (ext * PAD, total), 1)
        row, dx = at // PAD, at % PAD - (PAD - HALO if s == 0 else 0)
        source = half + (row - HALO) * HALO + dx
        fold_shift = jnp.where(north, half - HALO * HALO, 0)
        source = source + jnp.where(row >= rows + HALO, fold_shift, 0)
        keep = (lane == source) & (dx >= 0) & (dx < HALO)
        side[s] = dot(keep.astype(F32).astype(BF), table)

    def put_row(y, row, m):
        mask[y] = m
        shifted[y, :, c : 2 * c] = row.astype(BF)
        shifted[y, :, :c] = pltpu.roll(row, 1, 0).astype(BF)
        shifted[y, :, 2 * c :] = pltpu.roll(row, wide - 1, 0).astype(BF)

    def encoded_row(lanes, y):
        enc = dot(z[:, lanes], wenc_ref[...], TN)
        m = enc[:, c:]
        state = (activate(enc[:, :c]) * jnp.concatenate([m, m], 1)).astype(BF).astype(F32)
        at = pl.ds(y * PAD if isinstance(y, int) else pl.multiple_of(y * PAD, PAD), PAD)
        w, e = side[0, at, :], side[1, at, :]
        return (
            jnp.concatenate([w[:, :c], state, e[:, :c]], 0),
            jnp.concatenate([w[:, c:], m, e[:, c:]], 0),
        )

    def own_row(y, _):
        row, m = encoded_row(pl.ds(pl.multiple_of(y * LANES, LANES), LANES), y + HALO)
        put_row(y + HALO, row, m)
        return 0

    lax.fori_loop(0, rows, own_row, 0)
    for h in range(HALO):
        lo = cells + (HALO + h) * LANES
        put_row(h, *encoded_row(slice(lo, lo + LANES), h))
    above = []
    for h in range(HALO):
        lo = cells + h * LANES
        above.append(encoded_row(slice(lo, lo + LANES), rows + HALO + h))

    @pl.when(jnp.logical_not(north))
    def _():
        for h in range(HALO):
            put_row(rows + HALO + h, *above[h])

    @pl.when(north)
    def _():
        i0 = lax.broadcasted_iota(jnp.int32, (wide, wide), 0)
        i1 = lax.broadcasted_iota(jnp.int32, (wide, wide), 1)
        turn = (i0 + i1 == wide - 1).astype(F32).astype(BF)
        for h in range(HALO):
            row, m = above[HALO - 1 - h]
            put_row(rows + HALO + h, dot(turn, row.astype(BF)), dot(turn, m.astype(BF)))

    def mask_of(y, count, lo, size):
        m = mask[pl.ds(y, count), lo : lo + size, :].reshape(count * size, LANES)
        return jnp.concatenate([m, m], 1)

    def finish(y, count, conv):
        state = shifted[pl.ds(y, count), :, c : 2 * c].reshape(count * wide, c).astype(F32)
        state = mask_of(y, count, 0, wide) * (state + activate(conv))
        state = state.astype(BF).astype(F32)
        for q in range(count):
            row = state[q * wide : (q + 1) * wide]
            for k in range(3):
                moved = pltpu.roll(row, wide - (PAD - 1 + k), 0)[:LANES]
                shifted2[y - 1 + q, :, k * c : (k + 1) * c] = moved.astype(BF)

    step = 3

    def first(g, _):
        y = g * step + 1
        conv = None
        for a in range(3):
            lhs = shifted[pl.ds(y - 1 + a, step)].reshape(step * wide, 3 * c)
            term = dot(lhs, kw_ref[0, a * 3 * c : (a + 1) * 3 * c, :])
            conv = term if conv is None else conv + term
        finish(y, step, conv)
        return 0

    lax.fori_loop(0, (rows + 2) // step, first, 0)

    @pl.when(north)
    def _():
        y = rows + HALO
        conv = None
        for a in range(3):
            for b in range(3):
                lhs = shifted[y + 1 - a, :, (2 - b) * c : (3 - b) * c]
                at = (3 * a + b) * c
                term = dot(lhs, kw_ref[0, at : at + c, :])
                conv = term if conv is None else conv + term
        finish(y, 1, conv)

    step2 = 4

    def second(g, _):
        y = g * step2
        conv = None
        for a in range(3):
            lhs = shifted2[pl.ds(y + a, step2)].reshape(step2 * LANES, 3 * c)
            term = dot(lhs, kw_ref[1, a * 3 * c : (a + 1) * 3 * c, :])
            conv = term if conv is None else conv + term
        state = shifted2[pl.ds(y + 1, step2), :, c : 2 * c].reshape(step2 * LANES, c).astype(F32)
        state = mask_of(y + HALO, step2, PAD, LANES) * (state + activate(conv))
        got = dot(thermal_ref[...], state.astype(BF), NT)
        for q in range(step2):
            row = got[:1, q * LANES : (q + 1) * LANES]
            out_ref[pl.ds(y + q, 1), :] = row * sea_ref[pl.ds(y + q, 1), :].astype(F32)
        return 0

    lax.fori_loop(0, rows // step2, second, 0)


def per_device(
    air_condition_inputs,
    air_embedding_matrix,
    air_blending_matrix,
    exchange_readout_matrix,
    overlay_share_factors,
    marine_condition_inputs,
    water_embedding_matrix,
    drive_lifting_matrix,
    segment_stencil_factors,
    thermal_readout_matrix,
    water_point_indicator,
):
    n_lat, n_lon = lax.axis_size("lat"), lax.axis_size("lon")
    i, j = lax.axis_index("lat"), lax.axis_index("lon")
    bands, width, cells = overlay_share_factors.shape
    fields, rows, cols = marine_condition_inputs.shape
    afields = air_condition_inputs.shape[0]
    share = air_embedding_matrix.shape[1]
    chan = share * n_lon
    c = water_embedding_matrix.shape[1]
    where = jnp.stack([i % 2, (i == n_lat - 1).astype(jnp.int32)]).astype(jnp.int32)

    mine = jnp.concatenate(
        [
            air_blending_matrix.T,
            air_embedding_matrix.T,
            exchange_readout_matrix,
            jnp.zeros((share, LANES - 48 - 8), BF),
        ],
        1,
    )
    weights = lax.all_to_all(
        jnp.broadcast_to(mine[None], (n_lon, *mine.shape)), "lon", 0, 0, tiled=True
    ).reshape(chan, chan + LANES)

    marine = jnp.concatenate(
        [
            marine_condition_inputs.reshape(fields, cells),
            water_point_indicator.astype(BF).reshape(1, cells),
            jnp.zeros((MM - fields - 1, cells), BF),
        ],
        0,
    )
    edges = pl.pallas_call(
        edge_kernel,
        out_shape=[jax.ShapeDtypeStruct((HALO * rows, (bands + 1) * LANES), BF)] * 2,
        name="edges",
    )
    to_east, to_west = edges(overlay_share_factors, marine)
    east = [(k, (k + 1) % n_lon) for k in range(n_lon)]
    west = [(b, a) for a, b in east]
    from_west = lax.ppermute(to_east, "lon", east)
    from_east = lax.ppermute(to_west, "lon", west)

    tiles = []
    for d in (-1, 0, 1):
        at = (j + d + n_lon) % n_lon * width
        tile = lax.dynamic_slice_in_dim(air_condition_inputs, at, width, 2)
        tiles.append(jnp.pad(tile.reshape(afields, bands * width), ((0, 0), (0, TILE - bands * width))))
    air = jnp.concatenate(tiles, 1)

    size = bands * HALO * 96 + HALO * MM + (bands + 1) * HALO * rows + air.shape[1] // LANES * afields
    pack = pl.pallas_call(
        pack_kernel,
        in_specs=[pl.BlockSpec(memory_space=pltpu.SMEM)] + [pl.BlockSpec(memory_space=pltpu.VMEM)] * 5,
        out_shape=[jax.ShapeDtypeStruct((size, LANES), BF)] * 2,
        name="pack",
    )
    to_a, to_b = pack(where, overlay_share_factors, marine, from_west, from_east, air)
    pairs_a = [(k, k ^ 1) for k in range(n_lat)]
    pairs_b = []
    for k in range(1, n_lat):
        for m in range(n_lon):
            if k == n_lat - 1:
                other = k * n_lon + n_lon - 1 - m
            else:
                other = (((k - 1) ^ 1) + 1) * n_lon + m
            pairs_b.append((k * n_lon + m, other))
    from_a = lax.ppermute(to_a, "lat", pairs_a)
    from_b = lax.ppermute(to_b, ("lat", "lon"), pairs_b)

    encoder = jnp.concatenate(
        [
            jnp.pad(water_embedding_matrix, ((0, MM - fields), (0, LANES))),
            jnp.pad(drive_lifting_matrix, ((0, 8), (0, LANES))),
        ],
        0,
    )
    r0 = lax.broadcasted_iota(jnp.int32, encoder.shape, 0)
    r1 = lax.broadcasted_iota(jnp.int32, encoder.shape, 1)
    encoder = jnp.where((r0 == fields) & (r1 >= c), jnp.ones((), BF), encoder)
    thermal = jnp.broadcast_to(thermal_readout_matrix[None], (8, c))
    stencil = segment_stencil_factors.reshape(-1, 9 * c, c)

    wide, ext = cols + 2 * PAD, rows + 2 * HALO
    main = pl.pallas_call(
        main_kernel,
        in_specs=[pl.BlockSpec(memory_space=pltpu.SMEM)] + [pl.BlockSpec(memory_space=pltpu.VMEM)] * 12,
        out_shape=jax.ShapeDtypeStruct((rows, cols), F32),
        scratch_shapes=[
            pltpu.VMEM((9, afields, TILE), BF),
            pltpu.VMEM((9, 16, bands * LANES), BF),
            pltpu.VMEM((MM + 16, cells + 2 * HALO * LANES), BF),
            pltpu.VMEM((2, ext * PAD, c + LANES), F32),
            pltpu.VMEM((ext, wide, 3 * c), BF),
            pltpu.VMEM((ext - 2, cols, 3 * c), BF),
            pltpu.VMEM((ext, wide, LANES), F32),
        ],
        name="main",
    )
    return main(
        where, weights, air, from_a, from_b, from_west, from_east, overlay_share_factors, marine,
        water_point_indicator, encoder, stencil, thermal,
    )


def solution(mesh):
    return jax.shard_map(
        per_device,
        mesh=mesh,
        in_specs=(
            P(None, "lat", None),
            P(None, "lon"),
            P(None, "lon"),
            P("lon", None),
            P("lat", "lon", None),
            P(None, "lat", "lon"),
            P(),
            P(),
            P(),
            P(),
            P("lat", "lon"),
        ),
        out_specs=P("lat", "lon"),
        check_vma=False,
    )
```

```python
import jax
import jax.numpy as jnp
from jax import lax
from jax.experimental import pallas as pl
from jax.experimental.pallas import tpu as pltpu
from jax.sharding import PartitionSpec as P

BF = jnp.bfloat16
F32 = jnp.float32
LANES = 128
PAD = 8
HALO = 2
MM = 80
TILE = 384
NT = ((1,), (1,))
TN = ((0,), (0,))


def activate(values):
    inner = values * (0.7978845608028654 + 0.035677408136300125 * (values * values))
    half = 0.5 * values
    return half + half * jnp.tanh(inner)


def dot(a, b, dims=((1,), (0,))):
    return lax.dot_general(a, b, (dims, ((), ())), preferred_element_type=F32)


def one_hot(keep):
    return keep.astype(F32).astype(BF)


def weights_kernel(mix_ref, emb_ref, out_ref, all_ref):
    share, chan = mix_ref.shape
    for k in range(all_ref.shape[0]):
        all_ref[k, :, :chan] = mix_ref[...]
        all_ref[k, :, chan:] = jnp.zeros((share, LANES), BF)
        all_ref[k, :, chan : chan + emb_ref.shape[1]] = emb_ref[...]
    readout = out_ref[...].astype(F32).T.astype(BF)
    for k in range(all_ref.shape[0]):
        all_ref[k, :, chan + 48 : chan + 56] = readout


def edge_kernel(ov_ref, mm_ref, east_ref, west_ref):
    near, cells = ov_ref.shape
    n = HALO * cells // LANES
    which = lax.broadcasted_iota(jnp.int32, (2 * n, cells), 0)
    lane = lax.broadcasted_iota(jnp.int32, (2 * n, cells), 1)
    side = which // n
    inside = which % n
    target = (inside // HALO) * LANES + inside % HALO + side * (LANES - HALO)
    pick = one_hot(lane == target)
    east_ref[...] = jnp.zeros_like(east_ref)
    west_ref[...] = jnp.zeros_like(west_ref)
    got = dot(pick, ov_ref[...], NT).astype(BF)
    west_ref[:, :near] = got[:n]
    east_ref[:, :near] = got[n:]
    got = dot(pick, mm_ref[...], NT).astype(BF)
    west_ref[:, TILE : TILE + MM] = got[:n]
    east_ref[:, TILE : TILE + MM] = got[n:]


def pack_kernel(where_ref, lo_ref, hi_ref, mlo_ref, mhi_ref, rw_ref, re_ref, air_ref, a_ref, b_ref):
    near = lo_ref.shape[0]

    def write(dst, top):
        ov, mm = (hi_ref, mhi_ref) if top else (lo_ref, mlo_ref)
        half = rw_ref.shape[0] // 2
        edge = half if top else 0
        at = 0
        for h in range(HALO):
            lanes = slice(h * LANES, (h + 1) * LANES)
            dst[at : at + near, :] = ov[:, lanes]
            dst[at + near : at + near + MM, :] = mm[:, lanes]
            at += near + MM
        for q in range(rw_ref.shape[1] // LANES):
            lanes = slice(q * LANES, (q + 1) * LANES)
            dst[at : at + half, :] = rw_ref[edge : edge + half, lanes]
            dst[at + half : at + 2 * half, :] = re_ref[edge : edge + half, lanes]
            at += 2 * half
        for q in range(air_ref.shape[1] // LANES):
            dst[at : at + 48, :] = air_ref[:, q * LANES : (q + 1) * LANES]
            at += 48

    even = where_ref[0] == 0

    @pl.when(even)
    def _():
        write(a_ref, True)
        write(b_ref, False)

    @pl.when(jnp.logical_not(even))
    def _():
        write(a_ref, False)
        write(b_ref, True)


def atmosphere(wts_ref, airs, flux, tiles, bands, width):
    chan = wts_ref.shape[0]
    i0 = lax.broadcasted_iota(jnp.int32, (TILE, TILE), 0)
    i1 = lax.broadcasted_iota(jnp.int32, (TILE, TILE), 1)
    order = one_hot((i0 == (i1 % bands) * width + i1 // bands) & (i1 < bands * width))

    def tile(k, _):
        first = activate(dot(wts_ref[:, chan : chan + 48], airs[k])).astype(BF)
        second = activate(dot(wts_ref[:, :chan], first)).astype(BF)
        got = dot(wts_ref[:, chan : chan + LANES], second, TN)[48:56].astype(BF)
        got = dot(got, order)
        flux[k] = jnp.concatenate([got, jnp.ones_like(got)], 0).astype(BF)
        return 0

    lax.fori_loop(0, tiles, tile, 0)


def forced(sums):
    return sums[:8] / jnp.maximum(sums[8:], 0.25)


def fill(z, lanes, fields, sums):
    z[:MM, lanes] = fields
    z[MM:, lanes] = jnp.concatenate([forced(sums), jnp.zeros_like(sums[:8])], 0).astype(BF)


def edge_cells(table, flu, wenc_ref):
    c = wenc_ref.shape[1] - LANES
    weighted, coverage = dot(table[:, :TILE], flu[:8], NT), dot(table[:, :TILE], flu[8:], NT)
    forcing = (weighted / jnp.maximum(coverage, 0.25)).astype(BF)
    enc = dot(table[:, TILE : TILE + MM], wenc_ref[:MM])
    state = enc[:, :c] + dot(forcing, wenc_ref[MM : MM + 8, :c])
    m = enc[:, c:]
    state = activate(state) * jnp.concatenate([m, m], 1)
    return jnp.concatenate([state.astype(BF), m.astype(BF)], 1)


def encoded_row(z, lanes, wenc_ref, west, east):
    c = wenc_ref.shape[1] - LANES
    enc = dot(z[:, lanes], wenc_ref[...], TN)
    m = enc[:, c:]
    state = (activate(enc[:, :c]) * jnp.concatenate([m, m], 1)).astype(BF).astype(F32)
    return (
        jnp.concatenate([west[:, :c], state, east[:, :c]], 0),
        jnp.concatenate([west[:, c:], m, east[:, c:]], 0),
    )


def three_shifts(dst, row):
    c = row.shape[1]
    dst[:, c : 2 * c] = row.astype(BF)
    dst[:, :c] = pltpu.roll(row, 1, 0).astype(BF)
    dst[:, 2 * c :] = pltpu.roll(row, row.shape[0] - 1, 0).astype(BF)


def inner_shifts(dst, row):
    c = row.shape[1]
    for k in range(3):
        moved = pltpu.roll(row, row.shape[0] - (PAD - 1 + k), 0)[:LANES]
        dst[:, k * c : (k + 1) * c] = moved.astype(BF)


def taps(window, kernel):
    conv = None
    for a in range(3):
        lhs = window(a)
        term = dot(lhs, kernel[a * lhs.shape[1] : (a + 1) * lhs.shape[1], :])
        conv = term if conv is None else conv + term
    return conv


def section(state, m, conv):
    return jnp.concatenate([m, m], 1) * (state.astype(F32) + activate(conv))


def main1_kernel(
    wts_ref, air_ref, rw_ref, re_ref, ov_ref, mm_ref, sea_ref, wenc_ref, kw_ref, thermal_ref,
    mid_ref, s0_ref, m0_ref, s1_ref,
    airs, flux, z, side, shifted, shifted2, mask,
):
    near, cells = ov_ref.shape
    bands, width = BANDS, near // BANDS
    rows = cells // LANES
    c = kw_ref.shape[2]
    n = HALO * rows
    wide = LANES + 2 * PAD

    for k in range(3):
        airs[k] = air_ref[:, k * TILE : (k + 1) * TILE]
    atmosphere(wts_ref, airs, flux, 3, bands, width)
    fill(z, slice(0, cells), mm_ref[...], dot(flux[1, :, :near], ov_ref[...]))

    for s in range(2):
        table = edge_cells((rw_ref, re_ref)[s][...], flux[2 * s], wenc_ref)
        at = lax.broadcasted_iota(jnp.int32, (rows * PAD, n), 0)
        lane = lax.broadcasted_iota(jnp.int32, (rows * PAD, n), 1)
        dx = at % PAD - (PAD - HALO if s == 0 else 0)
        keep = (lane == at // PAD * HALO + dx) & (dx >= 0) & (dx < HALO)
        side[s] = dot(one_hot(keep), table)

    def own_row(y, _):
        lanes = pl.ds(pl.multiple_of(y * LANES, LANES), LANES)
        at = pl.ds(pl.multiple_of(y * PAD, PAD), PAD)
        row, m = encoded_row(z, lanes, wenc_ref, side[0, at, :], side[1, at, :])
        mask[y] = m
        three_shifts(shifted.at[y], row)
        return 0

    lax.fori_loop(0, rows, own_row, 0)
    step = 2

    def first(g, _):
        y = g * step + 1
        conv = taps(lambda a: shifted[pl.ds(y - 1 + a, step)].reshape(step * wide, 3 * c), kw_ref.at[0])
        state = shifted[pl.ds(y, step), :, c : 2 * c].reshape(step * wide, c)
        state = section(state, mask[pl.ds(y, step)].reshape(step * wide, LANES), conv)
        state = state.astype(BF).astype(F32)
        for q in range(step):
            inner_shifts(shifted2.at[y + q], state[q * wide : (q + 1) * wide])
        return 0

    lax.fori_loop(0, (rows - 2) // step, first, 0)
    step2 = 4

    def second(g, _):
        y = g * step2 + 2
        conv = taps(
            lambda a: shifted2[pl.ds(y - 1 + a, step2)].reshape(step2 * LANES, 3 * c), kw_ref.at[1]
        )
        state = shifted2[pl.ds(y, step2), :, c : 2 * c].reshape(step2 * LANES, c)
        m = mask[pl.ds(y, step2), PAD : PAD + LANES, :].reshape(step2 * LANES, LANES)
        got = dot(thermal_ref[...], section(state, m, conv).astype(BF), NT)
        for q in range(step2):
            row = got[:1, q * LANES : (q + 1) * LANES]
            mid_ref[pl.ds(y + q, 1), :] = row * sea_ref[pl.ds(y + q, 1), :].astype(F32)
        return 0

    lax.fori_loop(0, (rows - 4) // step2, second, 0)
    for q, y in enumerate((0, 1, rows - 2, rows - 1)):
        s0_ref[q] = shifted[y]
        m0_ref[q] = mask[y]
    for q, y in enumerate((1, 2, rows - 3, rows - 2)):
        s1_ref[q] = shifted2[y]


def main2_kernel(
    where_ref, wts_ref, pa_ref, pb_ref, mid_ref, s0_ref, m0_ref, s1_ref, sea_ref, wenc_ref, kw_ref, thermal_ref,
    out_ref,
    airs, flux, z, side, shifted, shifted2, mask,
):
    rows = out_ref.shape[0]
    near = NEAR
    bands, width = BANDS, near // BANDS
    c = kw_ref.shape[2]
    half = HALO * rows // 2
    wide = LANES + 2 * PAD
    even = where_ref[0] == 0
    north = where_ref[1] == 1
    at_edge = HALO * (near + MM)
    at_air = at_edge + (TILE + LANES) // LANES * 2 * half

    def halo(which, lo, size):
        a, b = pa_ref[lo : lo + size, :], pb_ref[lo : lo + size, :]
        return jnp.where(even, b, a) if which == 0 else jnp.where(even, a, b)

    for which in range(2):
        for k in range(3):
            for q in range(TILE // LANES):
                at = at_air + (k * (TILE // LANES) + q) * 48
                airs[3 * which + k, :, q * LANES : (q + 1) * LANES] = halo(which, at, 48)
    atmosphere(wts_ref, airs, flux, 6, bands, width)
    for which in range(2):
        for h in range(HALO):
            sums = dot(flux[3 * which + 1, :, :near], halo(which, h * (near + MM), near))
            at = (which * HALO + h) * LANES
            fill(z, slice(at, at + LANES), halo(which, h * (near + MM) + near, MM), sums)
    for s in range(2):
        parts = []
        for which in range(2):
            table = [
                halo(which, at_edge + q * 2 * half + s * half, half) for q in range((TILE + LANES) // LANES)
            ]
            parts.append(edge_cells(jnp.concatenate(table, 1), flux[3 * which + 2 * s], wenc_ref))
        table = jnp.concatenate(parts, 0)
        at = lax.broadcasted_iota(jnp.int32, (2 * HALO * PAD, 2 * half), 0)
        lane = lax.broadcasted_iota(jnp.int32, (2 * HALO * PAD, 2 * half), 1)
        row, dx = at // PAD, at % PAD - (PAD - HALO if s == 0 else 0)
        last = half - HALO * HALO
        source = jnp.where(
            row < HALO, last + row * HALO, half + (row - HALO) * HALO + jnp.where(north, last, 0)
        )
        keep = (lane == source + dx) & (dx >= 0) & (dx < HALO)
        side[s] = dot(one_hot(keep), table)

    new = []
    for q in range(2 * HALO):
        at = slice(q * PAD, (q + 1) * PAD)
        lanes = slice(q * LANES, (q + 1) * LANES)
        new.append(encoded_row(z, lanes, wenc_ref, side[0, at, :], side[1, at, :]))

    def put(strip, y, row, m):
        mask[strip, y] = m
        three_shifts(shifted.at[strip, y], row)

    for h in range(HALO):
        put(0, h, *new[h])
        shifted[0, HALO + h] = s0_ref[h]
        mask[0, HALO + h] = m0_ref[h]
        shifted[1, h] = s0_ref[HALO + h]
        mask[1, h] = m0_ref[HALO + h]
        shifted2[0, HALO + h] = s1_ref[h]
        shifted2[1, h] = s1_ref[HALO + h]

    @pl.when(jnp.logical_not(north))
    def _():
        for h in range(HALO):
            put(1, HALO + h, *new[HALO + h])

    @pl.when(north)
    def _():
        i0 = lax.broadcasted_iota(jnp.int32, (wide, wide), 0)
        i1 = lax.broadcasted_iota(jnp.int32, (wide, wide), 1)
        turn = one_hot(i0 + i1 == wide - 1)
        for h in range(HALO):
            row, m = new[2 * HALO - 1 - h]
            put(1, HALO + h, dot(turn, row.astype(BF)), dot(turn, m.astype(BF)))

    size = 2 * HALO * wide
    conv = taps(lambda a: shifted[:, a : a + HALO].reshape(size, 3 * c), kw_ref.at[0])
    state = shifted[:, 1 : 1 + HALO, :, c : 2 * c].reshape(size, c)
    state = section(state, mask[:, 1 : 1 + HALO].reshape(size, LANES), conv).astype(BF).astype(F32)
    for q in range(2 * HALO):
        strip, y = q // HALO, q % HALO
        inner_shifts(shifted2.at[strip, HALO * strip + y], state[q * wide : (q + 1) * wide])

    @pl.when(north)
    def _():
        conv = None
        for a in range(3):
            for b in range(3):
                lhs = shifted[1, 3 - a, :, (2 - b) * c : (3 - b) * c]
                at = (3 * a + b) * c
                term = dot(lhs, kw_ref[0, at : at + c, :])
                conv = term if conv is None else conv + term
        state = section(shifted[1, 2, :, c : 2 * c], mask[1, 2], conv).astype(BF).astype(F32)
        inner_shifts(shifted2.at[1, 3], state)

    size = 2 * HALO * LANES
    conv = taps(lambda a: shifted2[:, a : a + HALO].reshape(size, 3 * c), kw_ref.at[1])
    state = shifted2[:, 1 : 1 + HALO, :, c : 2 * c].reshape(size, c)
    inner = slice(PAD, PAD + LANES)
    m = jnp.concatenate([mask[0, HALO:, inner, :], mask[1, :HALO, inner, :]], 0).reshape(size, LANES)
    got = dot(thermal_ref[...], section(state, m, conv).astype(BF), NT)
    out_ref[...] = mid_ref[...]
    for q, y in enumerate((0, 1, rows - 2, rows - 1)):
        row = got[:1, q * LANES : (q + 1) * LANES]
        out_ref[y : y + 1, :] = row * sea_ref[y : y + 1, :].astype(F32)


BANDS = 4
NEAR = 360
VMEM = pl.BlockSpec(memory_space=pltpu.VMEM)
SMEM = pl.BlockSpec(memory_space=pltpu.SMEM)


def call_main1(args, rows, cols, c):
    wide = cols + 2 * PAD
    return pl.pallas_call(
        main1_kernel,
        in_specs=[VMEM] * 10,
        out_shape=[
            jax.ShapeDtypeStruct((rows, cols), F32),
            jax.ShapeDtypeStruct((4, wide, 3 * c), BF),
            jax.ShapeDtypeStruct((4, wide, LANES), F32),
            jax.ShapeDtypeStruct((4, cols, 3 * c), BF),
        ],
        scratch_shapes=[
            pltpu.VMEM((3, 48, TILE), BF),
            pltpu.VMEM((3, 16, TILE), BF),
            pltpu.VMEM((MM + 16, rows * cols), BF),
            pltpu.VMEM((2, rows * PAD, c + LANES), F32),
            pltpu.VMEM((rows, wide, 3 * c), BF),
            pltpu.VMEM((rows, cols, 3 * c), BF),
            pltpu.VMEM((rows, wide, LANES), F32),
        ],
        cost_estimate=pl.CostEstimate(flops=6_000_000_000, bytes_accessed=8_000_000, transcendentals=2_000_000),
        name="main1",
    )(*args)


def call_main2(args, rows, cols, c):
    wide = cols + 2 * PAD
    return pl.pallas_call(
        main2_kernel,
        in_specs=[SMEM] + [VMEM] * 11,
        out_shape=jax.ShapeDtypeStruct((rows, cols), F32),
        scratch_shapes=[
            pltpu.VMEM((6, 48, TILE), BF),
            pltpu.VMEM((6, 16, TILE), BF),
            pltpu.VMEM((MM + 16, 2 * HALO * cols), BF),
            pltpu.VMEM((2, 2 * HALO * PAD, c + LANES), F32),
            pltpu.VMEM((2, 2 * HALO, wide, 3 * c), BF),
            pltpu.VMEM((2, 2 * HALO, cols, 3 * c), BF),
            pltpu.VMEM((2, 2 * HALO, wide, LANES), F32),
        ],
        cost_estimate=pl.CostEstimate(flops=3_000_000_000, bytes_accessed=6_000_000, transcendentals=2_500_000),
        name="main2",
    )(*args)


def per_device(
    air_condition_inputs,
    air_embedding_matrix,
    air_blending_matrix,
    exchange_readout_matrix,
    overlay_share_factors,
    marine_condition_inputs,
    water_embedding_matrix,
    drive_lifting_matrix,
    segment_stencil_factors,
    thermal_readout_matrix,
    water_point_indicator,
):
    n_lat, n_lon = lax.axis_size("lat"), lax.axis_size("lon")
    i, j = lax.axis_index("lat"), lax.axis_index("lon")
    bands, width, cells = overlay_share_factors.shape
    fields, rows, cols = marine_condition_inputs.shape
    afields = air_condition_inputs.shape[0]
    share = air_embedding_matrix.shape[1]
    chan = share * n_lon
    near = bands * width
    c = water_embedding_matrix.shape[1]
    where = jnp.stack([i % 2, (i == n_lat - 1).astype(jnp.int32)]).astype(jnp.int32)

    mine = pl.pallas_call(
        weights_kernel,
        out_shape=jax.ShapeDtypeStruct((n_lon, share, chan + LANES), BF),
        name="weights",
    )(air_blending_matrix.T, air_embedding_matrix.T, exchange_readout_matrix.T)
    weights = lax.all_to_all(mine, "lon", 0, 0, tiled=True).reshape(chan, chan + LANES)

    overlay = overlay_share_factors.transpose(1, 0, 2).reshape(near, cells)
    marine = jnp.concatenate(
        [
            marine_condition_inputs.reshape(fields, cells),
            water_point_indicator.astype(BF).reshape(1, cells),
            jnp.zeros((MM - fields - 1, cells), BF),
        ],
        0,
    )
    edges = pl.pallas_call(
        edge_kernel,
        out_shape=[jax.ShapeDtypeStruct((HALO * rows, TILE + LANES), BF)] * 2,
        name="edges",
    )
    to_east, to_west = edges(overlay, marine)
    east = [(k, (k + 1) % n_lon) for k in range(n_lon)]
    west = [(b, a) for a, b in east]
    from_west = lax.ppermute(to_east, "lon", east)
    from_east = lax.ppermute(to_west, "lon", west)

    tiles = []
    for d in (-1, 0, 1):
        at = (j + d + n_lon) % n_lon * width
        tile = lax.dynamic_slice_in_dim(air_condition_inputs, at, width, 2)
        tiles.append(jnp.pad(tile.reshape(afields, near), ((0, 0), (0, TILE - near))))
    air = jnp.concatenate(tiles, 1)

    size = HALO * (near + MM) + (TILE + LANES) // LANES * HALO * rows + air.shape[1] // LANES * afields
    last = cells // (HALO * LANES) - 1
    ends = [
        pl.BlockSpec((d, HALO * LANES), lambda g, k=k: (0, k)) for d in (near, MM) for k in (0, last)
    ]
    whole = [
        pl.BlockSpec((HALO * rows, TILE + LANES), lambda g: (0, 0)),
        pl.BlockSpec((HALO * rows, TILE + LANES), lambda g: (0, 0)),
        pl.BlockSpec(air.shape, lambda g: (0, 0)),
    ]
    to_a, to_b = pl.pallas_call(
        pack_kernel,
        grid=(1,),
        in_specs=[SMEM] + ends + whole,
        out_specs=[pl.BlockSpec((size, LANES), lambda g: (0, 0))] * 2,
        out_shape=[jax.ShapeDtypeStruct((size, LANES), BF)] * 2,
        name="pack",
    )(where, overlay, overlay, marine, marine, from_west, from_east, air)
    pairs_a = [(k, k ^ 1) for k in range(n_lat)]
    pairs_b = []
    for k in range(1, n_lat):
        for m in range(n_lon):
            if k == n_lat - 1:
                other = k * n_lon + n_lon - 1 - m
            else:
                other = (((k - 1) ^ 1) + 1) * n_lon + m
            pairs_b.append((k * n_lon + m, other))
    from_a = lax.ppermute(to_a, "lat", pairs_a)
    from_b = lax.ppermute(to_b, ("lat", "lon"), pairs_b)

    encoder = jnp.concatenate(
        [
            jnp.pad(water_embedding_matrix, ((0, MM - fields), (0, LANES))),
            jnp.pad(drive_lifting_matrix, ((0, 8), (0, LANES))),
        ],
        0,
    )
    r0 = lax.broadcasted_iota(jnp.int32, encoder.shape, 0)
    r1 = lax.broadcasted_iota(jnp.int32, encoder.shape, 1)
    encoder = jnp.where((r0 == fields) & (r1 >= c), jnp.ones((), BF), encoder)
    thermal = jnp.broadcast_to(thermal_readout_matrix[None], (8, c))
    stencil = segment_stencil_factors.reshape(-1, 9 * c, c)
    sea = water_point_indicator

    mid, s0, m0, s1 = call_main1(
        (weights, air, from_west, from_east, overlay, marine, sea, encoder, stencil, thermal), rows, cols, c
    )
    return call_main2(
        (where, weights, from_a, from_b, mid, s0, m0, s1, sea, encoder, stencil, thermal), rows, cols, c
    )


def solution(mesh):
    return jax.shard_map(
        per_device,
        mesh=mesh,
        in_specs=(
            P(None, "lat", None),
            P(None, "lon"),
            P(None, "lon"),
            P("lon", None),
            P("lat", "lon", None),
            P(None, "lat", "lon"),
            P(),
            P(),
            P(),
            P(),
            P("lat", "lon"),
        ),
        out_specs=P("lat", "lon"),
        check_vma=False,
    )
```

```python
import jax
import jax.numpy as jnp
from jax import lax
from jax.experimental import pallas as pl
from jax.experimental.pallas import tpu as pltpu
from jax.sharding import PartitionSpec as P

BF = jnp.bfloat16
F32 = jnp.float32
LANES = 128
PAD = 8
HALO = 2
MM = 80
TILE = 384
NT = ((1,), (1,))
TN = ((0,), (0,))


def activate(values):
    inner = values * (0.7978845608028654 + 0.035677408136300125 * (values * values))
    half = 0.5 * values
    return half + half * jnp.tanh(inner)


def dot(a, b, dims=((1,), (0,))):
    return lax.dot_general(a, b, (dims, ((), ())), preferred_element_type=F32)


def one_hot(keep):
    return keep.astype(F32).astype(BF)


def weights_kernel(mix_ref, emb_ref, out_ref, all_ref):
    share, chan = mix_ref.shape
    for k in range(all_ref.shape[0]):
        all_ref[k, :, :chan] = mix_ref[...]
        all_ref[k, :, chan:] = jnp.zeros((share, LANES), BF)
        all_ref[k, :, chan : chan + emb_ref.shape[1]] = emb_ref[...]
    readout = out_ref[...].astype(F32).T.astype(BF)
    for k in range(all_ref.shape[0]):
        all_ref[k, :, chan + 48 : chan + 56] = readout


def edge_kernel(ov_ref, mm_ref, east_ref, west_ref):
    near, cells = ov_ref.shape
    n = HALO * cells // LANES
    which = lax.broadcasted_iota(jnp.int32, (2 * n, cells), 0)
    lane = lax.broadcasted_iota(jnp.int32, (2 * n, cells), 1)
    side = which // n
    inside = which % n
    target = (inside // HALO) * LANES + inside % HALO + side * (LANES - HALO)
    pick = one_hot(lane == target)
    east_ref[...] = jnp.zeros_like(east_ref)
    west_ref[...] = jnp.zeros_like(west_ref)
    got = dot(pick, ov_ref[...], NT).astype(BF)
    west_ref[:, :near] = got[:n]
    east_ref[:, :near] = got[n:]
    got = dot(pick, mm_ref[...], NT).astype(BF)
    west_ref[:, TILE : TILE + MM] = got[:n]
    east_ref[:, TILE : TILE + MM] = got[n:]


def pack_kernel(where_ref, lo_ref, hi_ref, mlo_ref, mhi_ref, rw_ref, re_ref, air_ref, a_ref, b_ref):
    near = lo_ref.shape[0]

    def write(dst, top):
        ov, mm = (hi_ref, mhi_ref) if top else (lo_ref, mlo_ref)
        half = rw_ref.shape[0] // 2
        edge = half if top else 0
        at = 0
        for h in range(HALO):
            lanes = slice(h * LANES, (h + 1) * LANES)
            dst[at : at + near, :] = ov[:, lanes]
            dst[at + near : at + near + MM, :] = mm[:, lanes]
            at += near + MM
        for q in range(rw_ref.shape[1] // LANES):
            lanes = slice(q * LANES, (q + 1) * LANES)
            dst[at : at + half, :] = rw_ref[edge : edge + half, lanes]
            dst[at + half : at + 2 * half, :] = re_ref[edge : edge + half, lanes]
            at += 2 * half
        for q in range(air_ref.shape[1] // LANES):
            dst[at : at + 48, :] = air_ref[:, q * LANES : (q + 1) * LANES]
            at += 48

    even = where_ref[0] == 0

    @pl.when(even)
    def _():
        write(a_ref, True)
        write(b_ref, False)

    @pl.when(jnp.logical_not(even))
    def _():
        write(a_ref, False)
        write(b_ref, True)


def atmosphere(wts_ref, airs, flux, groups, bands, width):
    chan = wts_ref.shape[0]
    i0 = lax.broadcasted_iota(jnp.int32, (TILE, TILE), 0)
    i1 = lax.broadcasted_iota(jnp.int32, (TILE, TILE), 1)
    order = one_hot((i0 == (i1 % bands) * width + i1 // bands) & (i1 < bands * width))

    def band(g, _):
        first = activate(dot(wts_ref[:, chan : chan + 48], airs[g])).astype(BF)
        second = activate(dot(wts_ref[:, :chan], first)).astype(BF)
        fluxes = dot(wts_ref[:, chan : chan + LANES], second, TN)[48:56].astype(BF)
        for k in range(3):
            got = dot(fluxes[:, k * TILE : (k + 1) * TILE], order)
            flux[3 * g + k] = jnp.concatenate([got, jnp.ones_like(got)], 0).astype(BF)
        return 0

    lax.fori_loop(0, groups, band, 0)


def forced(sums):
    return sums[:8] / jnp.maximum(sums[8:], 0.25)


def fill(z, lanes, fields, sums):
    z[:MM, lanes] = fields
    z[MM:, lanes] = jnp.concatenate([forced(sums), jnp.zeros_like(sums[:8])], 0).astype(BF)


def edge_cells(table, flu, wenc_ref):
    c = wenc_ref.shape[1] - LANES
    weighted, coverage = dot(table[:, :TILE], flu[:8], NT), dot(table[:, :TILE], flu[8:], NT)
    forcing = (weighted / jnp.maximum(coverage, 0.25)).astype(BF)
    enc = dot(table[:, TILE : TILE + MM], wenc_ref[:MM])
    state = enc[:, :c] + dot(forcing, wenc_ref[MM : MM + 8, :c])
    m = enc[:, c:]
    state = activate(state) * jnp.concatenate([m, m], 1)
    return jnp.concatenate([state.astype(BF), m.astype(BF)], 1)


def encoded_row(z, lanes, wenc_ref, west, east):
    c = wenc_ref.shape[1] - LANES
    enc = dot(z[:, lanes], wenc_ref[...], TN)
    m = enc[:, c:]
    state = (activate(enc[:, :c]) * jnp.concatenate([m, m], 1)).astype(BF).astype(F32)
    return (
        jnp.concatenate([west[:, :c], state, east[:, :c]], 0),
        jnp.concatenate([west[:, c:], m, east[:, c:]], 0),
    )


def three_shifts(dst, row):
    c = row.shape[1]
    dst[:, c : 2 * c] = row.astype(BF)
    dst[:, :c] = pltpu.roll(row, 1, 0).astype(BF)
    dst[:, 2 * c :] = pltpu.roll(row, row.shape[0] - 1, 0).astype(BF)


def inner_shifts(dst, row):
    c = row.shape[1]
    for k in range(3):
        moved = pltpu.roll(row, row.shape[0] - (PAD - 1 + k), 0)[:LANES]
        dst[:, k * c : (k + 1) * c] = moved.astype(BF)


def taps(window, kernel):
    conv = None
    for a in range(3):
        lhs = window(a)
        term = dot(lhs, kernel[a * lhs.shape[1] : (a + 1) * lhs.shape[1], :])
        conv = term if conv is None else conv + term
    return conv


def section(state, m, conv):
    return jnp.concatenate([m, m], 1) * (state.astype(F32) + activate(conv))


def main1_kernel(
    wts_ref, air_ref, rw_ref, re_ref, ov_ref, mm_ref, sea_ref, wenc_ref, kw_ref,
    mid_ref, s0_ref, m0_ref, s1_ref,
    airs, flux, z, side, shifted, shifted2, mask,
):
    near, cells = ov_ref.shape
    bands, width = BANDS, near // BANDS
    rows = cells // LANES
    c = kw_ref.shape[2]
    n = HALO * rows
    wide = LANES + 2 * PAD

    airs[0] = air_ref[...]
    atmosphere(wts_ref, airs, flux, 1, bands, width)
    fill(z, slice(0, cells), mm_ref[...], dot(flux[1, :, :near], ov_ref[...]))

    for s in range(2):
        table = edge_cells((rw_ref, re_ref)[s][...], flux[2 * s], wenc_ref)
        at = lax.broadcasted_iota(jnp.int32, (rows * PAD, n), 0)
        lane = lax.broadcasted_iota(jnp.int32, (rows * PAD, n), 1)
        dx = at % PAD - (PAD - HALO if s == 0 else 0)
        keep = (lane == at // PAD * HALO + dx) & (dx >= 0) & (dx < HALO)
        side[s] = dot(one_hot(keep), table)

    def own_row(y):
        lanes = pl.ds(pl.multiple_of(y * LANES, LANES), LANES)
        at = pl.ds(pl.multiple_of(y * PAD, PAD), PAD)
        row, m = encoded_row(z, lanes, wenc_ref, side[0, at, :], side[1, at, :])
        mask[y] = m
        three_shifts(shifted.at[y], row)

    together = 4

    def own_rows(g, _):
        for q in range(together):
            own_row(g * together + q)
        return 0

    lax.fori_loop(0, rows // together, own_rows, 0)
    step = 7

    def first(g, _):
        y = g * step + 1
        conv = taps(lambda a: shifted[pl.ds(y - 1 + a, step)].reshape(step * wide, 3 * c), kw_ref.at[0])
        state = shifted[pl.ds(y, step), :, c : 2 * c].reshape(step * wide, c)
        state = section(state, mask[pl.ds(y, step)].reshape(step * wide, LANES), conv)
        state = state.astype(BF).astype(F32)
        for q in range(step):
            inner_shifts(shifted2.at[y + q], state[q * wide : (q + 1) * wide])
        return 0

    lax.fori_loop(0, (rows - 2) // step, first, 0)
    step2 = 12

    def second(g, _):
        y = g * step2 + 2
        conv = taps(
            lambda a: shifted2[pl.ds(y - 1 + a, step2)].reshape(step2 * LANES, 3 * c), kw_ref.at[1]
        )
        state = shifted2[pl.ds(y, step2), :, c : 2 * c].reshape(step2 * LANES, c)
        m = mask[pl.ds(y, step2), PAD : PAD + LANES, :].reshape(step2 * LANES, LANES)
        got = dot(wenc_ref[MM + 8 :, :c], section(state, m, conv).astype(BF), NT)
        for q in range(step2):
            row = got[:1, q * LANES : (q + 1) * LANES]
            mid_ref[pl.ds(y + q, 1), :] = row * sea_ref[pl.ds(y + q, 1), :].astype(F32)
        return 0

    lax.fori_loop(0, (rows - 4) // step2, second, 0)
    for q, y in enumerate((0, 1, rows - 2, rows - 1)):
        s0_ref[q] = shifted[y]
        m0_ref[q] = mask[y]
    for q, y in enumerate((1, 2, rows - 3, rows - 2)):
        s1_ref[q] = shifted2[y]


def main2_kernel(
    where_ref, wts_ref, pa_ref, pb_ref, mid_ref, s0_ref, m0_ref, s1_ref, sea_ref, wenc_ref, kw_ref,
    out_ref,
    airs, flux, z, side, shifted, shifted2, mask,
):
    rows = out_ref.shape[0]
    near = NEAR
    bands, width = BANDS, near // BANDS
    c = kw_ref.shape[2]
    half = HALO * rows // 2
    wide = LANES + 2 * PAD
    even = where_ref[0] == 0
    north = where_ref[1] == 1
    at_edge = HALO * (near + MM)
    at_air = at_edge + (TILE + LANES) // LANES * 2 * half

    def halo(which, lo, size):
        a, b = pa_ref[lo : lo + size, :], pb_ref[lo : lo + size, :]
        return jnp.where(even, b, a) if which == 0 else jnp.where(even, a, b)

    for which in range(2):
        for q in range(3 * TILE // LANES):
            airs[which, :, q * LANES : (q + 1) * LANES] = halo(which, at_air + q * 48, 48)
    atmosphere(wts_ref, airs, flux, 2, bands, width)
    for which in range(2):
        for h in range(HALO):
            sums = dot(flux[3 * which + 1, :, :near], halo(which, h * (near + MM), near))
            at = (which * HALO + h) * LANES
            fill(z, slice(at, at + LANES), halo(which, h * (near + MM) + near, MM), sums)
    for s in range(2):
        parts = []
        for which in range(2):
            table = [
                halo(which, at_edge + q * 2 * half + s * half, half) for q in range((TILE + LANES) // LANES)
            ]
            parts.append(edge_cells(jnp.concatenate(table, 1), flux[3 * which + 2 * s], wenc_ref))
        table = jnp.concatenate(parts, 0)
        at = lax.broadcasted_iota(jnp.int32, (2 * HALO * PAD, 2 * half), 0)
        lane = lax.broadcasted_iota(jnp.int32, (2 * HALO * PAD, 2 * half), 1)
        row, dx = at // PAD, at % PAD - (PAD - HALO if s == 0 else 0)
        last = half - HALO * HALO
        source = jnp.where(
            row < HALO, last + row * HALO, half + (row - HALO) * HALO + jnp.where(north, last, 0)
        )
        keep = (lane == source + dx) & (dx >= 0) & (dx < HALO)
        side[s] = dot(one_hot(keep), table)

    new = []
    for q in range(2 * HALO):
        at = slice(q * PAD, (q + 1) * PAD)
        lanes = slice(q * LANES, (q + 1) * LANES)
        new.append(encoded_row(z, lanes, wenc_ref, side[0, at, :], side[1, at, :]))

    def put(strip, y, row, m):
        mask[strip, y] = m
        three_shifts(shifted.at[strip, y], row)

    for h in range(HALO):
        put(0, h, *new[h])
        shifted[0, HALO + h] = s0_ref[h]
        mask[0, HALO + h] = m0_ref[h]
        shifted[1, h] = s0_ref[HALO + h]
        mask[1, h] = m0_ref[HALO + h]
        shifted2[0, HALO + h] = s1_ref[h]
        shifted2[1, h] = s1_ref[HALO + h]

    @pl.when(jnp.logical_not(north))
    def _():
        for h in range(HALO):
            put(1, HALO + h, *new[HALO + h])

    @pl.when(north)
    def _():
        i0 = lax.broadcasted_iota(jnp.int32, (wide, wide), 0)
        i1 = lax.broadcasted_iota(jnp.int32, (wide, wide), 1)
        turn = one_hot(i0 + i1 == wide - 1)
        for h in range(HALO):
            row, m = new[2 * HALO - 1 - h]
            put(1, HALO + h, dot(turn, row.astype(BF)), dot(turn, m.astype(BF)))

    size = 2 * HALO * wide
    conv = taps(lambda a: shifted[:, a : a + HALO].reshape(size, 3 * c), kw_ref.at[0])
    state = shifted[:, 1 : 1 + HALO, :, c : 2 * c].reshape(size, c)
    state = section(state, mask[:, 1 : 1 + HALO].reshape(size, LANES), conv).astype(BF).astype(F32)
    for q in range(2 * HALO):
        strip, y = q // HALO, q % HALO
        inner_shifts(shifted2.at[strip, HALO * strip + y], state[q * wide : (q + 1) * wide])

    @pl.when(north)
    def _():
        conv = None
        for a in range(3):
            for b in range(3):
                lhs = shifted[1, 3 - a, :, (2 - b) * c : (3 - b) * c]
                at = (3 * a + b) * c
                term = dot(lhs, kw_ref[0, at : at + c, :])
                conv = term if conv is None else conv + term
        state = section(shifted[1, 2, :, c : 2 * c], mask[1, 2], conv).astype(BF).astype(F32)
        inner_shifts(shifted2.at[1, 3], state)

    size = 2 * HALO * LANES
    conv = taps(lambda a: shifted2[:, a : a + HALO].reshape(size, 3 * c), kw_ref.at[1])
    state = shifted2[:, 1 : 1 + HALO, :, c : 2 * c].reshape(size, c)
    inner = slice(PAD, PAD + LANES)
    m = jnp.concatenate([mask[0, HALO:, inner, :], mask[1, :HALO, inner, :]], 0).reshape(size, LANES)
    got = dot(wenc_ref[MM + 8 :, :c], section(state, m, conv).astype(BF), NT)
    out_ref[...] = mid_ref[...]
    for q, y in enumerate((0, 1, rows - 2, rows - 1)):
        row = got[:1, q * LANES : (q + 1) * LANES]
        out_ref[y : y + 1, :] = row * sea_ref[y : y + 1, :].astype(F32)


BANDS = 4
NEAR = 360
VMEM = pl.BlockSpec(memory_space=pltpu.VMEM)
SMEM = pl.BlockSpec(memory_space=pltpu.SMEM)


def call_main1(args, rows, cols, c):
    wide = cols + 2 * PAD
    return pl.pallas_call(
        main1_kernel,
        in_specs=[VMEM] * 9,
        out_shape=[
            jax.ShapeDtypeStruct((rows, cols), F32),
            jax.ShapeDtypeStruct((4, wide, 3 * c), BF),
            jax.ShapeDtypeStruct((4, wide, LANES), F32),
            jax.ShapeDtypeStruct((4, cols, 3 * c), BF),
        ],
        scratch_shapes=[
            pltpu.VMEM((1, 48, 3 * TILE), BF),
            pltpu.VMEM((3, 16, TILE), BF),
            pltpu.VMEM((MM + 16, rows * cols), BF),
            pltpu.VMEM((2, rows * PAD, c + LANES), F32),
            pltpu.VMEM((rows, wide, 3 * c), BF),
            pltpu.VMEM((rows, cols, 3 * c), BF),
            pltpu.VMEM((rows, wide, LANES), F32),
        ],
        cost_estimate=pl.CostEstimate(flops=6_000_000_000, bytes_accessed=8_000_000, transcendentals=2_000_000),
        name="main1",
        compiler_params=pltpu.CompilerParams(vmem_limit_bytes=30 << 20),
    )(*args)


def call_main2(args, rows, cols, c):
    wide = cols + 2 * PAD
    return pl.pallas_call(
        main2_kernel,
        in_specs=[SMEM] + [VMEM] * 10,
        out_shape=jax.ShapeDtypeStruct((rows, cols), F32),
        scratch_shapes=[
            pltpu.VMEM((2, 48, 3 * TILE), BF),
            pltpu.VMEM((6, 16, TILE), BF),
            pltpu.VMEM((MM + 16, 2 * HALO * cols), BF),
            pltpu.VMEM((2, 2 * HALO * PAD, c + LANES), F32),
            pltpu.VMEM((2, 2 * HALO, wide, 3 * c), BF),
            pltpu.VMEM((2, 2 * HALO, cols, 3 * c), BF),
            pltpu.VMEM((2, 2 * HALO, wide, LANES), F32),
        ],
        cost_estimate=pl.CostEstimate(flops=3_000_000_000, bytes_accessed=6_000_000, transcendentals=2_500_000),
        name="main2",
        compiler_params=pltpu.CompilerParams(vmem_limit_bytes=24 << 20),
    )(*args)


def per_device(
    air_condition_inputs,
    air_embedding_matrix,
    air_blending_matrix,
    exchange_readout_matrix,
    overlay_share_factors,
    marine_condition_inputs,
    water_embedding_matrix,
    drive_lifting_matrix,
    segment_stencil_factors,
    thermal_readout_matrix,
    water_point_indicator,
):
    n_lat, n_lon = lax.axis_size("lat"), lax.axis_size("lon")
    i, j = lax.axis_index("lat"), lax.axis_index("lon")
    bands, width, cells = overlay_share_factors.shape
    fields, rows, cols = marine_condition_inputs.shape
    afields = air_condition_inputs.shape[0]
    share = air_embedding_matrix.shape[1]
    chan = share * n_lon
    near = bands * width
    c = water_embedding_matrix.shape[1]
    where = jnp.stack([i % 2, (i == n_lat - 1).astype(jnp.int32)]).astype(jnp.int32)

    mine = pl.pallas_call(
        weights_kernel,
        out_shape=jax.ShapeDtypeStruct((n_lon, share, chan + LANES), BF),
        name="weights",
        compiler_params=pltpu.CompilerParams(vmem_limit_bytes=16 << 20),
    )(air_blending_matrix.T, air_embedding_matrix.T, exchange_readout_matrix.T)
    weights = lax.all_to_all(mine, "lon", 0, 0, tiled=True).reshape(chan, chan + LANES)

    overlay = overlay_share_factors.transpose(1, 0, 2).reshape(near, cells)
    marine = jnp.concatenate(
        [
            marine_condition_inputs.reshape(fields, cells),
            water_point_indicator.astype(BF).reshape(1, cells),
            jnp.zeros((MM - fields - 1, cells), BF),
        ],
        0,
    )
    edges = pl.pallas_call(
        edge_kernel,
        out_shape=[jax.ShapeDtypeStruct((HALO * rows, TILE + LANES), BF)] * 2,
        name="edges",
        compiler_params=pltpu.CompilerParams(vmem_limit_bytes=16 << 20),
    )
    to_east, to_west = edges(overlay, marine)
    east = [(k, (k + 1) % n_lon) for k in range(n_lon)]
    west = [(b, a) for a, b in east]
    from_west = lax.ppermute(to_east, "lon", east)
    from_east = lax.ppermute(to_west, "lon", west)

    tiles = []
    for d in (-1, 0, 1):
        at = (j + d + n_lon) % n_lon * width
        tile = lax.dynamic_slice_in_dim(air_condition_inputs, at, width, 2)
        tiles.append(jnp.pad(tile.reshape(afields, near), ((0, 0), (0, TILE - near))))
    air = jnp.concatenate(tiles, 1)

    size = HALO * (near + MM) + (TILE + LANES) // LANES * HALO * rows + air.shape[1] // LANES * afields
    last = cells // (HALO * LANES) - 1
    ends = [
        pl.BlockSpec((d, HALO * LANES), lambda g, k=k: (0, k)) for d in (near, MM) for k in (0, last)
    ]
    whole = [
        pl.BlockSpec((HALO * rows, TILE + LANES), lambda g: (0, 0)),
        pl.BlockSpec((HALO * rows, TILE + LANES), lambda g: (0, 0)),
        pl.BlockSpec(air.shape, lambda g: (0, 0)),
    ]
    to_a, to_b = pl.pallas_call(
        pack_kernel,
        grid=(1,),
        in_specs=[SMEM] + ends + whole,
        out_specs=[pl.BlockSpec((size, LANES), lambda g: (0, 0))] * 2,
        out_shape=[jax.ShapeDtypeStruct((size, LANES), BF)] * 2,
        name="pack",
        compiler_params=pltpu.CompilerParams(vmem_limit_bytes=16 << 20),
    )(where, overlay, overlay, marine, marine, from_west, from_east, air)
    pairs_a = [(k, k ^ 1) for k in range(n_lat)]
    pairs_b = []
    for k in range(1, n_lat):
        for m in range(n_lon):
            if k == n_lat - 1:
                other = k * n_lon + n_lon - 1 - m
            else:
                other = (((k - 1) ^ 1) + 1) * n_lon + m
            pairs_b.append((k * n_lon + m, other))
    from_a = lax.ppermute(to_a, "lat", pairs_a)
    from_b = lax.ppermute(to_b, ("lat", "lon"), pairs_b)

    encoder = jnp.concatenate(
        [
            jnp.pad(water_embedding_matrix, ((0, MM - fields), (0, LANES))),
            jnp.pad(drive_lifting_matrix, ((0, 0), (0, LANES))),
            jnp.pad(jnp.broadcast_to(thermal_readout_matrix[None], (8, c)), ((0, 0), (0, LANES))),
        ],
        0,
    )
    r0 = lax.broadcasted_iota(jnp.int32, encoder.shape, 0)
    r1 = lax.broadcasted_iota(jnp.int32, encoder.shape, 1)
    encoder = jnp.where((r0 == fields) & (r1 >= c), jnp.ones((), BF), encoder)
    stencil = segment_stencil_factors.reshape(-1, 9 * c, c)
    sea = water_point_indicator

    mid, s0, m0, s1 = call_main1(
        (weights, air, from_west, from_east, overlay, marine, sea, encoder, stencil), rows, cols, c
    )
    return call_main2(
        (where, weights, from_a, from_b, mid, s0, m0, s1, sea, encoder, stencil), rows, cols, c
    )


def solution(mesh):
    return jax.shard_map(
        per_device,
        mesh=mesh,
        in_specs=(
            P(None, "lat", None),
            P(None, "lon"),
            P(None, "lon"),
            P("lon", None),
            P("lat", "lon", None),
            P(None, "lat", "lon"),
            P(),
            P(),
            P(),
            P(),
            P("lat", "lon"),
        ),
        out_specs=P("lat", "lon"),
        check_vma=False,
    )
```

```python
import jax
import jax.numpy as jnp
from jax import lax
from jax.experimental import pallas as pl
from jax.experimental.pallas import tpu as pltpu
from jax.sharding import PartitionSpec as P

BF = jnp.bfloat16
F32 = jnp.float32
LANES = 128
PAD = 8
HALO = 2
MM = 80
TILE = 384
NT = ((1,), (1,))
TN = ((0,), (0,))


def activate(values):
    inner = values * (0.7978845608028654 + 0.035677408136300125 * (values * values))
    half = 0.5 * values
    return half + half * jnp.tanh(inner)


def in_hbm(value):
    return pltpu.with_memory_space_constraint(value, pltpu.HBM)


def dot(a, b, dims=((1,), (0,))):
    return lax.dot_general(a, b, (dims, ((), ())), preferred_element_type=F32)


def one_hot(keep):
    return keep.astype(F32).astype(BF)


def weights_kernel(mix_hbm, emb_hbm, out_hbm, all_ref, mix_ref, emb_ref, out_ref, sems):
    share, chan = mix_ref.shape
    pairs = ((mix_hbm, mix_ref), (emb_hbm, emb_ref), (out_hbm, out_ref))
    copies = [pltpu.make_async_copy(src, dst, sems.at[k]) for k, (src, dst) in enumerate(pairs)]
    for copy in copies:
        copy.start()
    for copy in copies:
        copy.wait()
    for k in range(all_ref.shape[0]):
        all_ref[k, :, :chan] = mix_ref[...]
        all_ref[k, :, chan:] = jnp.zeros((share, LANES), BF)
        all_ref[k, :, chan : chan + emb_ref.shape[1]] = emb_ref[...]
    readout = out_ref[...].astype(F32).T.astype(BF)
    for k in range(all_ref.shape[0]):
        all_ref[k, :, chan + 48 : chan + 56] = readout


def edge_kernel(where_ref, native_ref, mm_ref, ov_ref, a_ref, b_ref):
    near, cells = ov_ref.shape
    ov_ref[...] = native_ref[...].reshape(near, cells)
    n = HALO * cells // LANES
    which = lax.broadcasted_iota(jnp.int32, (2 * n, cells), 0)
    lane = lax.broadcasted_iota(jnp.int32, (2 * n, cells), 1)
    odd = where_ref[2] == 1
    east = (which < n) != odd
    inside = which % n
    target = (inside // HALO) * LANES + inside % HALO + jnp.where(east, LANES - HALO, 0)
    pick = one_hot(lane == target)
    a_ref[...] = jnp.zeros_like(a_ref)
    b_ref[...] = jnp.zeros_like(b_ref)
    got = dot(pick, ov_ref[...], NT).astype(BF)
    a_ref[:, :near] = got[:n]
    b_ref[:, :near] = got[n:]
    got = dot(pick, mm_ref[...], NT).astype(BF)
    a_ref[:, TILE : TILE + MM] = got[:n]
    b_ref[:, TILE : TILE + MM] = got[n:]


def pack_kernel(where_ref, lo_ref, hi_ref, mlo_ref, mhi_ref, ea_ref, eb_ref, air_ref, a_ref, b_ref):
    near = lo_ref.shape[0]
    odd = where_ref[2] == 1

    def write(dst, top):
        ov, mm = (hi_ref, mhi_ref) if top else (lo_ref, mlo_ref)
        half = ea_ref.shape[0] // 2
        edge = half if top else 0
        at = 0
        for h in range(HALO):
            lanes = slice(h * LANES, (h + 1) * LANES)
            dst[at : at + near, :] = ov[:, lanes]
            dst[at + near : at + near + MM, :] = mm[:, lanes]
            at += near + MM
        for q in range(ea_ref.shape[1] // LANES):
            lanes = slice(q * LANES, (q + 1) * LANES)
            a, b = ea_ref[edge : edge + half, lanes], eb_ref[edge : edge + half, lanes]
            dst[at : at + half, :] = jnp.where(odd, a, b)
            dst[at + half : at + 2 * half, :] = jnp.where(odd, b, a)
            at += 2 * half
        for q in range(air_ref.shape[1] // LANES):
            dst[at : at + 48, :] = air_ref[:, q * LANES : (q + 1) * LANES]
            at += 48

    even = where_ref[0] == 0

    @pl.when(even)
    def _():
        write(a_ref, True)
        write(b_ref, False)

    @pl.when(jnp.logical_not(even))
    def _():
        write(a_ref, False)
        write(b_ref, True)


def atmosphere(wts_ref, airs, flux, groups, bands, width):
    chan = wts_ref.shape[0]
    i0 = lax.broadcasted_iota(jnp.int32, (TILE, TILE), 0)
    i1 = lax.broadcasted_iota(jnp.int32, (TILE, TILE), 1)
    order = one_hot((i0 == (i1 % bands) * width + i1 // bands) & (i1 < bands * width))

    def band(g, _):
        first = activate(dot(wts_ref[:, chan : chan + 48], airs[g])).astype(BF)
        second = activate(dot(wts_ref[:, :chan], first)).astype(BF)
        fluxes = dot(wts_ref[:, chan : chan + LANES], second, TN)[48:56].astype(BF)
        for k in range(3):
            got = dot(fluxes[:, k * TILE : (k + 1) * TILE], order)
            flux[3 * g + k] = jnp.concatenate([got, jnp.ones_like(got)], 0).astype(BF)
        return 0

    lax.fori_loop(0, groups, band, 0)


def forced(sums):
    return sums[:8] / jnp.maximum(sums[8:], 0.25)


def fill(z, lanes, fields, sums):
    z[:MM, lanes] = fields
    z[MM:, lanes] = jnp.concatenate([forced(sums), jnp.zeros_like(sums[:8])], 0).astype(BF)


def edge_cells(table, flu, wenc_ref):
    c = wenc_ref.shape[1] - LANES
    weighted, coverage = dot(table[:, :TILE], flu[:8], NT), dot(table[:, :TILE], flu[8:], NT)
    forcing = (weighted / jnp.maximum(coverage, 0.25)).astype(BF)
    enc = dot(table[:, TILE : TILE + MM], wenc_ref[:MM])
    state = enc[:, :c] + dot(forcing, wenc_ref[MM : MM + 8, :c])
    m = enc[:, c:]
    state = activate(state) * jnp.concatenate([m, m], 1)
    return jnp.concatenate([state.astype(BF), m.astype(BF)], 1)


def encoded_row(z, lanes, wenc_ref, west, east):
    c = wenc_ref.shape[1] - LANES
    enc = dot(z[:, lanes], wenc_ref[...], TN)
    m = enc[:, c:]
    state = (activate(enc[:, :c]) * jnp.concatenate([m, m], 1)).astype(BF).astype(F32)
    return (
        jnp.concatenate([west[:, :c], state, east[:, :c]], 0),
        jnp.concatenate([west[:, c:], m, east[:, c:]], 0),
    )


def three_shifts(dst, row):
    c = row.shape[1]
    dst[:, c : 2 * c] = row.astype(BF)
    dst[:, :c] = pltpu.roll(row, 1, 0).astype(BF)
    dst[:, 2 * c :] = pltpu.roll(row, row.shape[0] - 1, 0).astype(BF)


def inner_shifts(dst, row):
    c = row.shape[1]
    for k in range(3):
        moved = pltpu.roll(row, row.shape[0] - (PAD - 1 + k), 0)[:LANES]
        dst[:, k * c : (k + 1) * c] = moved.astype(BF)


def taps(window, kernel):
    conv = None
    for a in range(3):
        lhs = window(a)
        term = dot(lhs, kernel[a * lhs.shape[1] : (a + 1) * lhs.shape[1], :])
        conv = term if conv is None else conv + term
    return conv


def section(state, m, conv):
    return jnp.concatenate([m, m], 1) * (state.astype(F32) + activate(conv))


def main1_kernel(
    where_ref, wts_ref, air_ref, ea_ref, eb_ref, ov_ref, mm_ref, sea_ref, wenc_ref, kw_hbm,
    mid_ref, s0_ref, m0_ref, s1_ref,
    airs, flux, z, side, shifted, shifted2, mask, kw_ref, sems,
):
    near, cells = ov_ref.shape
    bands, width = BANDS, near // BANDS
    rows = cells // LANES
    c = kw_ref.shape[2]
    n = HALO * rows
    wide = LANES + 2 * PAD
    odd = where_ref[2] == 1
    copies = [pltpu.make_async_copy(kw_hbm.at[k], kw_ref.at[k], sems.at[k]) for k in range(2)]
    for copy in copies:
        copy.start()

    airs[0] = air_ref[...]
    atmosphere(wts_ref, airs, flux, 1, bands, width)
    fill(z, slice(0, cells), mm_ref[...], dot(flux[1, :, :near], ov_ref[...]))

    for s in range(2):
        a, b = ea_ref[...], eb_ref[...]
        table = jnp.where(odd, a, b) if s == 0 else jnp.where(odd, b, a)
        table = edge_cells(table, flux[2 * s], wenc_ref)
        at = lax.broadcasted_iota(jnp.int32, (rows * PAD, n), 0)
        lane = lax.broadcasted_iota(jnp.int32, (rows * PAD, n), 1)
        dx = at % PAD - (PAD - HALO if s == 0 else 0)
        keep = (lane == at // PAD * HALO + dx) & (dx >= 0) & (dx < HALO)
        side[s] = dot(one_hot(keep), table)

    def own_row(y):
        lanes = pl.ds(pl.multiple_of(y * LANES, LANES), LANES)
        at = pl.ds(pl.multiple_of(y * PAD, PAD), PAD)
        row, m = encoded_row(z, lanes, wenc_ref, side[0, at, :], side[1, at, :])
        mask[y] = m
        three_shifts(shifted.at[y], row)

    together = 4

    def own_rows(g, _):
        for q in range(together):
            own_row(g * together + q)
        return 0

    lax.fori_loop(0, rows // together, own_rows, 0)
    step = 7

    def first(g, _):
        y = g * step + 1
        conv = taps(lambda a: shifted[pl.ds(y - 1 + a, step)].reshape(step * wide, 3 * c), kw_ref.at[0])
        state = shifted[pl.ds(y, step), :, c : 2 * c].reshape(step * wide, c)
        state = section(state, mask[pl.ds(y, step)].reshape(step * wide, LANES), conv)
        state = state.astype(BF).astype(F32)
        for q in range(step):
            inner_shifts(shifted2.at[y + q], state[q * wide : (q + 1) * wide])
        return 0

    copies[0].wait()
    lax.fori_loop(0, (rows - 2) // step, first, 0)
    step2 = 12

    def second(g, _):
        y = g * step2 + 2
        conv = taps(
            lambda a: shifted2[pl.ds(y - 1 + a, step2)].reshape(step2 * LANES, 3 * c), kw_ref.at[1]
        )
        state = shifted2[pl.ds(y, step2), :, c : 2 * c].reshape(step2 * LANES, c)
        m = mask[pl.ds(y, step2), PAD : PAD + LANES, :].reshape(step2 * LANES, LANES)
        got = dot(wenc_ref[MM + 8 :, :c], section(state, m, conv).astype(BF), NT)
        for q in range(step2):
            row = got[:1, q * LANES : (q + 1) * LANES]
            mid_ref[pl.ds(y + q, 1), :] = row * sea_ref[pl.ds(y + q, 1), :].astype(F32)
        return 0

    copies[1].wait()
    lax.fori_loop(0, (rows - 4) // step2, second, 0)
    for q, y in enumerate((0, 1, rows - 2, rows - 1)):
        s0_ref[q] = shifted[y]
        m0_ref[q] = mask[y]
    for q, y in enumerate((1, 2, rows - 3, rows - 2)):
        s1_ref[q] = shifted2[y]


def main2_kernel(
    where_ref, wts_ref, pa_ref, pb_ref, mid_ref, s0_ref, m0_ref, s1_ref, sea_ref, wenc_ref, kw_hbm,
    out_ref,
    airs, flux, z, side, shifted, shifted2, mask, kw_ref, sems,
):
    rows = out_ref.shape[0]
    near = NEAR
    bands, width = BANDS, near // BANDS
    c = kw_ref.shape[2]
    half = HALO * rows // 2
    wide = LANES + 2 * PAD
    even = where_ref[0] == 0
    north = where_ref[1] == 1
    at_edge = HALO * (near + MM)
    at_air = at_edge + (TILE + LANES) // LANES * 2 * half
    copies = [pltpu.make_async_copy(kw_hbm.at[k], kw_ref.at[k], sems.at[k]) for k in range(2)]
    for copy in copies:
        copy.start()

    def halo(which, lo, size):
        a, b = pa_ref[lo : lo + size, :], pb_ref[lo : lo + size, :]
        return jnp.where(even, b, a) if which == 0 else jnp.where(even, a, b)

    for which in range(2):
        for q in range(3 * TILE // LANES):
            airs[which, :, q * LANES : (q + 1) * LANES] = halo(which, at_air + q * 48, 48)
    atmosphere(wts_ref, airs, flux, 2, bands, width)
    for which in range(2):
        for h in range(HALO):
            sums = dot(flux[3 * which + 1, :, :near], halo(which, h * (near + MM), near))
            at = (which * HALO + h) * LANES
            fill(z, slice(at, at + LANES), halo(which, h * (near + MM) + near, MM), sums)
    for s in range(2):
        parts = []
        for which in range(2):
            table = [
                halo(which, at_edge + q * 2 * half + s * half, half) for q in range((TILE + LANES) // LANES)
            ]
            parts.append(edge_cells(jnp.concatenate(table, 1), flux[3 * which + 2 * s], wenc_ref))
        table = jnp.concatenate(parts, 0)
        at = lax.broadcasted_iota(jnp.int32, (2 * HALO * PAD, 2 * half), 0)
        lane = lax.broadcasted_iota(jnp.int32, (2 * HALO * PAD, 2 * half), 1)
        row, dx = at // PAD, at % PAD - (PAD - HALO if s == 0 else 0)
        last = half - HALO * HALO
        source = jnp.where(
            row < HALO, last + row * HALO, half + (row - HALO) * HALO + jnp.where(north, last, 0)
        )
        keep = (lane == source + dx) & (dx >= 0) & (dx < HALO)
        side[s] = dot(one_hot(keep), table)

    new = []
    for q in range(2 * HALO):
        at = slice(q * PAD, (q + 1) * PAD)
        lanes = slice(q * LANES, (q + 1) * LANES)
        new.append(encoded_row(z, lanes, wenc_ref, side[0, at, :], side[1, at, :]))

    def put(strip, y, row, m):
        mask[strip, y] = m
        three_shifts(shifted.at[strip, y], row)

    for h in range(HALO):
        put(0, h, *new[h])
        shifted[0, HALO + h] = s0_ref[h]
        mask[0, HALO + h] = m0_ref[h]
        shifted[1, h] = s0_ref[HALO + h]
        mask[1, h] = m0_ref[HALO + h]
        shifted2[0, HALO + h] = s1_ref[h]
        shifted2[1, h] = s1_ref[HALO + h]

    @pl.when(jnp.logical_not(north))
    def _():
        for h in range(HALO):
            put(1, HALO + h, *new[HALO + h])

    @pl.when(north)
    def _():
        i0 = lax.broadcasted_iota(jnp.int32, (wide, wide), 0)
        i1 = lax.broadcasted_iota(jnp.int32, (wide, wide), 1)
        turn = one_hot(i0 + i1 == wide - 1)
        for h in range(HALO):
            row, m = new[2 * HALO - 1 - h]
            put(1, HALO + h, dot(turn, row.astype(BF)), dot(turn, m.astype(BF)))

    copies[0].wait()
    size = 2 * HALO * wide
    conv = taps(lambda a: shifted[:, a : a + HALO].reshape(size, 3 * c), kw_ref.at[0])
    state = shifted[:, 1 : 1 + HALO, :, c : 2 * c].reshape(size, c)
    state = section(state, mask[:, 1 : 1 + HALO].reshape(size, LANES), conv).astype(BF).astype(F32)
    for q in range(2 * HALO):
        strip, y = q // HALO, q % HALO
        inner_shifts(shifted2.at[strip, HALO * strip + y], state[q * wide : (q + 1) * wide])

    @pl.when(north)
    def _():
        conv = None
        for a in range(3):
            for b in range(3):
                lhs = shifted[1, 3 - a, :, (2 - b) * c : (3 - b) * c]
                at = (3 * a + b) * c
                term = dot(lhs, kw_ref[0, at : at + c, :])
                conv = term if conv is None else conv + term
        state = section(shifted[1, 2, :, c : 2 * c], mask[1, 2], conv).astype(BF).astype(F32)
        inner_shifts(shifted2.at[1, 3], state)

    copies[1].wait()
    size = 2 * HALO * LANES
    conv = taps(lambda a: shifted2[:, a : a + HALO].reshape(size, 3 * c), kw_ref.at[1])
    state = shifted2[:, 1 : 1 + HALO, :, c : 2 * c].reshape(size, c)
    inner = slice(PAD, PAD + LANES)
    m = jnp.concatenate([mask[0, HALO:, inner, :], mask[1, :HALO, inner, :]], 0).reshape(size, LANES)
    got = dot(wenc_ref[MM + 8 :, :c], section(state, m, conv).astype(BF), NT)
    out_ref[...] = mid_ref[...]
    for q, y in enumerate((0, 1, rows - 2, rows - 1)):
        row = got[:1, q * LANES : (q + 1) * LANES]
        out_ref[y : y + 1, :] = row * sea_ref[y : y + 1, :].astype(F32)


BANDS = 4
NEAR = 360
VMEM = pl.BlockSpec(memory_space=pltpu.VMEM)
SMEM = pl.BlockSpec(memory_space=pltpu.SMEM)
HBM = pl.BlockSpec(memory_space=pltpu.HBM)


def call_main1(args, rows, cols, c):
    wide = cols + 2 * PAD
    return pl.pallas_call(
        main1_kernel,
        in_specs=[SMEM] + [VMEM] * 8 + [HBM],
        out_shape=[
            jax.ShapeDtypeStruct((rows, cols), F32),
            jax.ShapeDtypeStruct((4, wide, 3 * c), BF),
            jax.ShapeDtypeStruct((4, wide, LANES), F32),
            jax.ShapeDtypeStruct((4, cols, 3 * c), BF),
        ],
        scratch_shapes=[
            pltpu.VMEM((1, 48, 3 * TILE), BF),
            pltpu.VMEM((3, 16, TILE), BF),
            pltpu.VMEM((MM + 16, rows * cols), BF),
            pltpu.VMEM((2, rows * PAD, c + LANES), F32),
            pltpu.VMEM((rows, wide, 3 * c), BF),
            pltpu.VMEM((rows, cols, 3 * c), BF),
            pltpu.VMEM((rows, wide, LANES), F32),
            pltpu.VMEM(args[-1].shape, BF),
            pltpu.SemaphoreType.DMA((2,)),
        ],
        cost_estimate=pl.CostEstimate(flops=6_000_000_000, bytes_accessed=8_000_000, transcendentals=2_000_000),
        name="main1",
        compiler_params=pltpu.CompilerParams(vmem_limit_bytes=30 << 20),
    )(*args)


def call_main2(args, rows, cols, c):
    wide = cols + 2 * PAD
    return pl.pallas_call(
        main2_kernel,
        in_specs=[SMEM] + [VMEM] * 9 + [HBM],
        out_shape=jax.ShapeDtypeStruct((rows, cols), F32),
        scratch_shapes=[
            pltpu.VMEM((2, 48, 3 * TILE), BF),
            pltpu.VMEM((6, 16, TILE), BF),
            pltpu.VMEM((MM + 16, 2 * HALO * cols), BF),
            pltpu.VMEM((2, 2 * HALO * PAD, c + LANES), F32),
            pltpu.VMEM((2, 2 * HALO, wide, 3 * c), BF),
            pltpu.VMEM((2, 2 * HALO, cols, 3 * c), BF),
            pltpu.VMEM((2, 2 * HALO, wide, LANES), F32),
            pltpu.VMEM(args[-1].shape, BF),
            pltpu.SemaphoreType.DMA((2,)),
        ],
        cost_estimate=pl.CostEstimate(flops=3_000_000_000, bytes_accessed=6_000_000, transcendentals=2_500_000),
        name="main2",
        compiler_params=pltpu.CompilerParams(vmem_limit_bytes=24 << 20),
    )(*args)


def per_device(
    air_condition_inputs,
    air_embedding_matrix,
    air_blending_matrix,
    exchange_readout_matrix,
    overlay_share_factors,
    marine_condition_inputs,
    water_embedding_matrix,
    drive_lifting_matrix,
    segment_stencil_factors,
    thermal_readout_matrix,
    water_point_indicator,
):
    n_lat, n_lon = lax.axis_size("lat"), lax.axis_size("lon")
    i, j = lax.axis_index("lat"), lax.axis_index("lon")
    bands, width, cells = overlay_share_factors.shape
    fields, rows, cols = marine_condition_inputs.shape
    afields = air_condition_inputs.shape[0]
    share = air_embedding_matrix.shape[1]
    chan = share * n_lon
    near = bands * width
    c = water_embedding_matrix.shape[1]
    where = jnp.stack([i % 2, (i == n_lat - 1).astype(jnp.int32), j % 2]).astype(jnp.int32)

    mine = pl.pallas_call(
        weights_kernel,
        in_specs=[HBM] * 3,
        scratch_shapes=[
            pltpu.VMEM((share, chan), BF),
            pltpu.VMEM((share, afields), BF),
            pltpu.VMEM((exchange_readout_matrix.shape[1], share), BF),
            pltpu.SemaphoreType.DMA((3,)),
        ],
        out_shape=jax.ShapeDtypeStruct((n_lon, share, chan + LANES), BF),
        name="weights",
        compiler_params=pltpu.CompilerParams(vmem_limit_bytes=16 << 20),
    )(*map(in_hbm, (air_blending_matrix.T, air_embedding_matrix.T, exchange_readout_matrix.T)))
    weights = lax.all_to_all(mine, "lon", 0, 0, tiled=True).reshape(chan, chan + LANES)

    marine = jnp.concatenate(
        [
            marine_condition_inputs.reshape(fields, cells),
            water_point_indicator.astype(BF).reshape(1, cells),
            jnp.zeros((MM - fields - 1, cells), BF),
        ],
        0,
    )
    edges = pl.pallas_call(
        edge_kernel,
        in_specs=[SMEM, VMEM, VMEM],
        out_shape=[jax.ShapeDtypeStruct((near, cells), BF)]
        + [jax.ShapeDtypeStruct((HALO * rows, TILE + LANES), BF)] * 2,
        name="edges",
        compiler_params=pltpu.CompilerParams(vmem_limit_bytes=16 << 20),
    )
    overlay, edge_a, edge_b = edges(where, overlay_share_factors.transpose(1, 0, 2), marine)
    pairs_b = [(k, ((k - 1) % n_lon ^ 1) + 1) for k in range(n_lon)]
    edge_b = lax.ppermute(edge_b, "lon", [(k, m % n_lon) for k, m in pairs_b])
    edge_a = lax.ppermute(edge_a, "lon", [(k, k ^ 1) for k in range(n_lon)])

    tiles = []
    for d in (-1, 0, 1):
        at = (j + d + n_lon) % n_lon * width
        tile = lax.dynamic_slice_in_dim(air_condition_inputs, at, width, 2)
        tiles.append(jnp.pad(tile.reshape(afields, near), ((0, 0), (0, TILE - near))))
    air = jnp.concatenate(tiles, 1)

    size = HALO * (near + MM) + (TILE + LANES) // LANES * HALO * rows + air.shape[1] // LANES * afields
    last = cells // (HALO * LANES) - 1
    ends = [
        pl.BlockSpec((d, HALO * LANES), lambda g, k=k: (0, k)) for d in (near, MM) for k in (0, last)
    ]
    whole = [
        pl.BlockSpec((HALO * rows, TILE + LANES), lambda g: (0, 0)),
        pl.BlockSpec((HALO * rows, TILE + LANES), lambda g: (0, 0)),
        pl.BlockSpec(air.shape, lambda g: (0, 0)),
    ]
    to_a, to_b = pl.pallas_call(
        pack_kernel,
        grid=(1,),
        in_specs=[SMEM] + ends + whole,
        out_specs=[pl.BlockSpec((size, LANES), lambda g: (0, 0))] * 2,
        out_shape=[jax.ShapeDtypeStruct((size, LANES), BF)] * 2,
        name="pack",
        compiler_params=pltpu.CompilerParams(vmem_limit_bytes=16 << 20),
    )(where, overlay, overlay, marine, marine, edge_a, edge_b, air)
    pairs_a = [(k, k ^ 1) for k in range(n_lat)]
    pairs_b = []
    for k in range(1, n_lat):
        for m in range(n_lon):
            if k == n_lat - 1:
                other = k * n_lon + n_lon - 1 - m
            else:
                other = (((k - 1) ^ 1) + 1) * n_lon + m
            pairs_b.append((k * n_lon + m, other))
    from_a = lax.ppermute(to_a, "lat", pairs_a)
    from_b = lax.ppermute(to_b, ("lat", "lon"), pairs_b)

    encoder = jnp.concatenate(
        [
            jnp.pad(water_embedding_matrix, ((0, MM - fields), (0, LANES))),
            jnp.pad(drive_lifting_matrix, ((0, 0), (0, LANES))),
            jnp.pad(jnp.broadcast_to(thermal_readout_matrix[None], (8, c)), ((0, 0), (0, LANES))),
        ],
        0,
    )
    r0 = lax.broadcasted_iota(jnp.int32, encoder.shape, 0)
    r1 = lax.broadcasted_iota(jnp.int32, encoder.shape, 1)
    encoder = jnp.where((r0 == fields) & (r1 >= c), jnp.ones((), BF), encoder)
    stencil = in_hbm(segment_stencil_factors.reshape(-1, 9 * c, c))
    sea = water_point_indicator

    mid, s0, m0, s1 = call_main1(
        (where, weights, air, edge_a, edge_b, overlay, marine, sea, encoder, stencil), rows, cols, c
    )
    return call_main2(
        (where, weights, from_a, from_b, mid, s0, m0, s1, sea, encoder, stencil), rows, cols, c
    )


def solution(mesh):
    return jax.shard_map(
        per_device,
        mesh=mesh,
        in_specs=(
            P(None, "lat", None),
            P(None, "lon"),
            P(None, "lon"),
            P("lon", None),
            P("lat", "lon", None),
            P(None, "lat", "lon"),
            P(),
            P(),
            P(),
            P(),
            P("lat", "lon"),
        ),
        out_specs=P("lat", "lon"),
        check_vma=False,
    )
```

```python
import jax
import jax.numpy as jnp
from jax import lax
from jax.experimental import pallas as pl
from jax.experimental.pallas import tpu as pltpu
from jax.sharding import PartitionSpec as P

BF = jnp.bfloat16
F32 = jnp.float32
LANES = 128
PAD = 8
HALO = 2
MM = 80
TILE = 384
NT = ((1,), (1,))
TN = ((0,), (0,))


def activate(values):
    inner = values * (0.7978845608028654 + 0.035677408136300125 * (values * values))
    half = 0.5 * values
    return half + half * jnp.tanh(inner)


def in_hbm(value):
    return pltpu.with_memory_space_constraint(value, pltpu.HBM)


def dot(a, b, dims=((1,), (0,))):
    return lax.dot_general(a, b, (dims, ((), ())), preferred_element_type=F32)


def one_hot(keep):
    return keep.astype(F32).astype(BF)


def weights_kernel(mix_hbm, emb_hbm, out_hbm, all_ref, mix_ref, emb_ref, out_ref, sems):
    share, chan = mix_ref.shape
    pairs = ((mix_hbm, mix_ref), (emb_hbm, emb_ref), (out_hbm, out_ref))
    copies = [pltpu.make_async_copy(src, dst, sems.at[k]) for k, (src, dst) in enumerate(pairs)]
    for copy in copies:
        copy.start()
    for copy in copies:
        copy.wait()
    for k in range(all_ref.shape[0]):
        all_ref[k, :, :chan] = mix_ref[...]
        all_ref[k, :, chan:] = jnp.zeros((share, LANES), BF)
        all_ref[k, :, chan : chan + emb_ref.shape[1]] = emb_ref[...]
    readout = out_ref[...].astype(F32).T.astype(BF)
    for k in range(all_ref.shape[0]):
        all_ref[k, :, chan + 48 : chan + 56] = readout


def edge_kernel(where_ref, native_hbm, mm_ref, ov_ref, a_ref, b_ref, native_ref, sems):
    near, cells = ov_ref.shape
    chunks = sems.shape[0]
    size = native_ref.shape[0] // chunks
    copies = []
    for k in range(chunks):
        at = slice(k * size, (k + 1) * size)
        copies.append(pltpu.make_async_copy(native_hbm.at[at], native_ref.at[at], sems.at[k]))
        copies[-1].start()
    n = HALO * cells // LANES
    which = lax.broadcasted_iota(jnp.int32, (2 * n, cells), 0)
    lane = lax.broadcasted_iota(jnp.int32, (2 * n, cells), 1)
    odd = where_ref[2] == 1
    east = (which < n) != odd
    inside = which % n
    target = (inside // HALO) * LANES + inside % HALO + jnp.where(east, LANES - HALO, 0)
    pick = one_hot(lane == target)
    for k, copy in enumerate(copies):
        copy.wait()
        rows = near // chunks
        part = native_ref[k * size : (k + 1) * size].reshape(rows, cells)
        ov_ref[k * rows : (k + 1) * rows, :] = part
    a_ref[...] = jnp.zeros_like(a_ref)
    b_ref[...] = jnp.zeros_like(b_ref)
    got = dot(pick, ov_ref[...], NT).astype(BF)
    a_ref[:, :near] = got[:n]
    b_ref[:, :near] = got[n:]
    got = dot(pick, mm_ref[...], NT).astype(BF)
    a_ref[:, TILE : TILE + MM] = got[:n]
    b_ref[:, TILE : TILE + MM] = got[n:]


def pack_kernel(where_ref, lo_ref, hi_ref, mlo_ref, mhi_ref, ea_ref, eb_ref, flux_ref, a_ref, b_ref):
    near = lo_ref.shape[0]
    odd = where_ref[2] == 1

    def write(dst, top):
        ov, mm = (hi_ref, mhi_ref) if top else (lo_ref, mlo_ref)
        half = ea_ref.shape[0] // 2
        edge = half if top else 0
        at = 0
        for h in range(HALO):
            lanes = slice(h * LANES, (h + 1) * LANES)
            dst[at : at + near, :] = ov[:, lanes]
            dst[at + near : at + near + MM, :] = mm[:, lanes]
            at += near + MM
        for q in range(ea_ref.shape[1] // LANES):
            lanes = slice(q * LANES, (q + 1) * LANES)
            a, b = ea_ref[edge : edge + half, lanes], eb_ref[edge : edge + half, lanes]
            dst[at : at + half, :] = jnp.where(odd, a, b)
            dst[at + half : at + 2 * half, :] = jnp.where(odd, b, a)
            at += 2 * half
        for k in range(3):
            for q in range(TILE // LANES):
                dst[at : at + 16, :] = flux_ref[k, :, q * LANES : (q + 1) * LANES]
                at += 16

    even = where_ref[0] == 0

    @pl.when(even)
    def _():
        write(a_ref, True)
        write(b_ref, False)

    @pl.when(jnp.logical_not(even))
    def _():
        write(a_ref, False)
        write(b_ref, True)


def own_band_kernel(wts_ref, air_ref, flux):
    chan = wts_ref.shape[0]
    width = NEAR // BANDS
    i0 = lax.broadcasted_iota(jnp.int32, (TILE, TILE), 0)
    i1 = lax.broadcasted_iota(jnp.int32, (TILE, TILE), 1)
    order = one_hot((i0 == (i1 % BANDS) * width + i1 // BANDS) & (i1 < NEAR))
    first = activate(dot(wts_ref[:, chan : chan + 48], air_ref[...])).astype(BF)
    second = activate(dot(wts_ref[:, :chan], first)).astype(BF)
    fluxes = dot(wts_ref[:, chan : chan + LANES], second, TN)[48:56].astype(BF)
    for k in range(3):
        got = dot(fluxes[:, k * TILE : (k + 1) * TILE], order)
        flux[k] = jnp.concatenate([got, jnp.ones_like(got)], 0).astype(BF)


def forced(sums):
    return sums[:8] / jnp.maximum(sums[8:], 0.25)


def fill(z, lanes, fields, sums):
    z[:MM, lanes] = fields
    z[MM:, lanes] = jnp.concatenate([forced(sums), jnp.zeros_like(sums[:8])], 0).astype(BF)


def edge_cells(table, flu, wenc_ref):
    c = wenc_ref.shape[1] - LANES
    weighted, coverage = dot(table[:, :TILE], flu[:8], NT), dot(table[:, :TILE], flu[8:], NT)
    forcing = (weighted / jnp.maximum(coverage, 0.25)).astype(BF)
    enc = dot(table[:, TILE : TILE + MM], wenc_ref[:MM])
    state = enc[:, :c] + dot(forcing, wenc_ref[MM : MM + 8, :c])
    m = enc[:, c:]
    state = activate(state) * jnp.concatenate([m, m], 1)
    return jnp.concatenate([state.astype(BF), m.astype(BF)], 1)


def encoded_row(z, lanes, wenc_ref, west, east):
    c = wenc_ref.shape[1] - LANES
    enc = dot(z[:, lanes], wenc_ref[...], TN)
    m = enc[:, c:]
    state = (activate(enc[:, :c]) * jnp.concatenate([m, m], 1)).astype(BF).astype(F32)
    return (
        jnp.concatenate([west[:, :c], state, east[:, :c]], 0),
        jnp.concatenate([west[:, c:], m, east[:, c:]], 0),
    )


def three_shifts(dst, row):
    c = row.shape[1]
    dst[:, c : 2 * c] = row.astype(BF)
    dst[:, :c] = pltpu.roll(row, 1, 0).astype(BF)
    dst[:, 2 * c :] = pltpu.roll(row, row.shape[0] - 1, 0).astype(BF)


def inner_shifts(dst, row):
    c = row.shape[1]
    for k in range(3):
        moved = pltpu.roll(row, row.shape[0] - (PAD - 1 + k), 0)[:LANES]
        dst[:, k * c : (k + 1) * c] = moved.astype(BF)


def taps(window, kernel):
    conv = None
    for a in range(3):
        lhs = window(a)
        term = dot(lhs, kernel[a * lhs.shape[1] : (a + 1) * lhs.shape[1], :])
        conv = term if conv is None else conv + term
    return conv


def section(state, m, conv):
    return jnp.concatenate([m, m], 1) * (state.astype(F32) + activate(conv))


def main1_kernel(
    where_ref, flux, ea_ref, eb_ref, ov_ref, mm_ref, sea_ref, wenc_ref, kw_hbm,
    mid_ref, s0_ref, m0_ref, s1_ref,
    z, side, shifted, shifted2, mask, kw_ref, sems,
):
    near, cells = ov_ref.shape
    rows = cells // LANES
    c = kw_ref.shape[2]
    n = HALO * rows
    wide = LANES + 2 * PAD
    odd = where_ref[2] == 1
    copies = [pltpu.make_async_copy(kw_hbm.at[k], kw_ref.at[k], sems.at[k]) for k in range(2)]
    for copy in copies:
        copy.start()

    fill(z, slice(0, cells), mm_ref[...], dot(flux[1, :, :near], ov_ref[...]))

    for s in range(2):
        a, b = ea_ref[...], eb_ref[...]
        table = jnp.where(odd, a, b) if s == 0 else jnp.where(odd, b, a)
        table = edge_cells(table, flux[2 * s], wenc_ref)
        at = lax.broadcasted_iota(jnp.int32, (rows * PAD, n), 0)
        lane = lax.broadcasted_iota(jnp.int32, (rows * PAD, n), 1)
        dx = at % PAD - (PAD - HALO if s == 0 else 0)
        keep = (lane == at // PAD * HALO + dx) & (dx >= 0) & (dx < HALO)
        side[s] = dot(one_hot(keep), table)

    def own_row(y):
        lanes = pl.ds(pl.multiple_of(y * LANES, LANES), LANES)
        at = pl.ds(pl.multiple_of(y * PAD, PAD), PAD)
        row, m = encoded_row(z, lanes, wenc_ref, side[0, at, :], side[1, at, :])
        mask[y] = m
        three_shifts(shifted.at[y], row)

    together = 4

    def own_rows(g, _):
        for q in range(together):
            own_row(g * together + q)
        return 0

    lax.fori_loop(0, rows // together, own_rows, 0)
    step = 7

    def first(g, _):
        y = g * step + 1
        conv = taps(lambda a: shifted[pl.ds(y - 1 + a, step)].reshape(step * wide, 3 * c), kw_ref.at[0])
        state = shifted[pl.ds(y, step), :, c : 2 * c].reshape(step * wide, c)
        state = section(state, mask[pl.ds(y, step)].reshape(step * wide, LANES), conv)
        state = state.astype(BF).astype(F32)
        for q in range(step):
            inner_shifts(shifted2.at[y + q], state[q * wide : (q + 1) * wide])
        return 0

    copies[0].wait()
    lax.fori_loop(0, (rows - 2) // step, first, 0)
    step2 = 12

    def second(g, _):
        y = g * step2 + 2
        conv = taps(
            lambda a: shifted2[pl.ds(y - 1 + a, step2)].reshape(step2 * LANES, 3 * c), kw_ref.at[1]
        )
        state = shifted2[pl.ds(y, step2), :, c : 2 * c].reshape(step2 * LANES, c)
        m = mask[pl.ds(y, step2), PAD : PAD + LANES, :].reshape(step2 * LANES, LANES)
        got = dot(wenc_ref[MM + 8 :, :c], section(state, m, conv).astype(BF), NT)
        for q in range(step2):
            row = got[:1, q * LANES : (q + 1) * LANES]
            mid_ref[pl.ds(y + q, 1), :] = row * sea_ref[pl.ds(y + q, 1), :].astype(F32)
        return 0

    copies[1].wait()
    lax.fori_loop(0, (rows - 4) // step2, second, 0)
    for q, y in enumerate((0, 1, rows - 2, rows - 1)):
        s0_ref[q] = shifted[y]
        m0_ref[q] = mask[y]
    for q, y in enumerate((1, 2, rows - 3, rows - 2)):
        s1_ref[q] = shifted2[y]


def main2_kernel(
    where_ref, pa_ref, pb_ref, mid_ref, s0_ref, m0_ref, s1_ref, sea_ref, wenc_ref, kw_hbm,
    out_ref,
    flux, z, side, shifted, shifted2, mask, kw_ref, sems,
):
    rows = out_ref.shape[0]
    near = NEAR
    c = kw_ref.shape[2]
    half = HALO * rows // 2
    wide = LANES + 2 * PAD
    even = where_ref[0] == 0
    north = where_ref[1] == 1
    at_edge = HALO * (near + MM)
    at_flux = at_edge + (TILE + LANES) // LANES * 2 * half
    copies = [pltpu.make_async_copy(kw_hbm.at[k], kw_ref.at[k], sems.at[k]) for k in range(2)]
    for copy in copies:
        copy.start()

    def halo(which, lo, size):
        a, b = pa_ref[lo : lo + size, :], pb_ref[lo : lo + size, :]
        return jnp.where(even, b, a) if which == 0 else jnp.where(even, a, b)

    for which in range(2):
        for k in range(3):
            for q in range(TILE // LANES):
                at = at_flux + (k * (TILE // LANES) + q) * 16
                flux[3 * which + k, :, q * LANES : (q + 1) * LANES] = halo(which, at, 16)
    for which in range(2):
        for h in range(HALO):
            sums = dot(flux[3 * which + 1, :, :near], halo(which, h * (near + MM), near))
            at = (which * HALO + h) * LANES
            fill(z, slice(at, at + LANES), halo(which, h * (near + MM) + near, MM), sums)
    for s in range(2):
        parts = []
        for which in range(2):
            table = [
                halo(which, at_edge + q * 2 * half + s * half, half) for q in range((TILE + LANES) // LANES)
            ]
            parts.append(edge_cells(jnp.concatenate(table, 1), flux[3 * which + 2 * s], wenc_ref))
        table = jnp.concatenate(parts, 0)
        at = lax.broadcasted_iota(jnp.int32, (2 * HALO * PAD, 2 * half), 0)
        lane = lax.broadcasted_iota(jnp.int32, (2 * HALO * PAD, 2 * half), 1)
        row, dx = at // PAD, at % PAD - (PAD - HALO if s == 0 else 0)
        last = half - HALO * HALO
        source = jnp.where(
            row < HALO, last + row * HALO, half + (row - HALO) * HALO + jnp.where(north, last, 0)
        )
        keep = (lane == source + dx) & (dx >= 0) & (dx < HALO)
        side[s] = dot(one_hot(keep), table)

    new = []
    for q in range(2 * HALO):
        at = slice(q * PAD, (q + 1) * PAD)
        lanes = slice(q * LANES, (q + 1) * LANES)
        new.append(encoded_row(z, lanes, wenc_ref, side[0, at, :], side[1, at, :]))

    def put(strip, y, row, m):
        mask[strip, y] = m
        three_shifts(shifted.at[strip, y], row)

    for h in range(HALO):
        put(0, h, *new[h])
        shifted[0, HALO + h] = s0_ref[h]
        mask[0, HALO + h] = m0_ref[h]
        shifted[1, h] = s0_ref[HALO + h]
        mask[1, h] = m0_ref[HALO + h]
        shifted2[0, HALO + h] = s1_ref[h]
        shifted2[1, h] = s1_ref[HALO + h]

    @pl.when(jnp.logical_not(north))
    def _():
        for h in range(HALO):
            put(1, HALO + h, *new[HALO + h])

    @pl.when(north)
    def _():
        i0 = lax.broadcasted_iota(jnp.int32, (wide, wide), 0)
        i1 = lax.broadcasted_iota(jnp.int32, (wide, wide), 1)
        turn = one_hot(i0 + i1 == wide - 1)
        for h in range(HALO):
            row, m = new[2 * HALO - 1 - h]
            put(1, HALO + h, dot(turn, row.astype(BF)), dot(turn, m.astype(BF)))

    copies[0].wait()
    size = 2 * HALO * wide
    conv = taps(lambda a: shifted[:, a : a + HALO].reshape(size, 3 * c), kw_ref.at[0])
    state = shifted[:, 1 : 1 + HALO, :, c : 2 * c].reshape(size, c)
    state = section(state, mask[:, 1 : 1 + HALO].reshape(size, LANES), conv).astype(BF).astype(F32)
    for q in range(2 * HALO):
        strip, y = q // HALO, q % HALO
        inner_shifts(shifted2.at[strip, HALO * strip + y], state[q * wide : (q + 1) * wide])

    @pl.when(north)
    def _():
        conv = None
        for a in range(3):
            for b in range(3):
                lhs = shifted[1, 3 - a, :, (2 - b) * c : (3 - b) * c]
                at = (3 * a + b) * c
                term = dot(lhs, kw_ref[0, at : at + c, :])
                conv = term if conv is None else conv + term
        state = section(shifted[1, 2, :, c : 2 * c], mask[1, 2], conv).astype(BF).astype(F32)
        inner_shifts(shifted2.at[1, 3], state)

    copies[1].wait()
    size = 2 * HALO * LANES
    conv = taps(lambda a: shifted2[:, a : a + HALO].reshape(size, 3 * c), kw_ref.at[1])
    state = shifted2[:, 1 : 1 + HALO, :, c : 2 * c].reshape(size, c)
    inner = slice(PAD, PAD + LANES)
    m = jnp.concatenate([mask[0, HALO:, inner, :], mask[1, :HALO, inner, :]], 0).reshape(size, LANES)
    got = dot(wenc_ref[MM + 8 :, :c], section(state, m, conv).astype(BF), NT)
    out_ref[...] = mid_ref[...]
    for q, y in enumerate((0, 1, rows - 2, rows - 1)):
        row = got[:1, q * LANES : (q + 1) * LANES]
        out_ref[y : y + 1, :] = row * sea_ref[y : y + 1, :].astype(F32)


BANDS = 4
NEAR = 360
VMEM = pl.BlockSpec(memory_space=pltpu.VMEM)
SMEM = pl.BlockSpec(memory_space=pltpu.SMEM)
HBM = pl.BlockSpec(memory_space=pltpu.HBM)


def call_main1(args, rows, cols, c):
    wide = cols + 2 * PAD
    return pl.pallas_call(
        main1_kernel,
        in_specs=[SMEM] + [VMEM] * 7 + [HBM],
        out_shape=[
            jax.ShapeDtypeStruct((rows, cols), F32),
            jax.ShapeDtypeStruct((4, wide, 3 * c), BF),
            jax.ShapeDtypeStruct((4, wide, LANES), F32),
            jax.ShapeDtypeStruct((4, cols, 3 * c), BF),
        ],
        scratch_shapes=[
            pltpu.VMEM((MM + 16, rows * cols), BF),
            pltpu.VMEM((2, rows * PAD, c + LANES), F32),
            pltpu.VMEM((rows, wide, 3 * c), BF),
            pltpu.VMEM((rows, cols, 3 * c), BF),
            pltpu.VMEM((rows, wide, LANES), F32),
            pltpu.VMEM(args[-1].shape, BF),
            pltpu.SemaphoreType.DMA((2,)),
        ],
        cost_estimate=pl.CostEstimate(flops=6_000_000_000, bytes_accessed=8_000_000, transcendentals=2_000_000),
        name="main1",
        compiler_params=pltpu.CompilerParams(vmem_limit_bytes=30 << 20),
    )(*args)


def call_main2(args, rows, cols, c):
    wide = cols + 2 * PAD
    return pl.pallas_call(
        main2_kernel,
        in_specs=[SMEM] + [VMEM] * 8 + [HBM],
        out_shape=jax.ShapeDtypeStruct((rows, cols), F32),
        scratch_shapes=[
            pltpu.VMEM((6, 16, TILE), BF),
            pltpu.VMEM((MM + 16, 2 * HALO * cols), BF),
            pltpu.VMEM((2, 2 * HALO * PAD, c + LANES), F32),
            pltpu.VMEM((2, 2 * HALO, wide, 3 * c), BF),
            pltpu.VMEM((2, 2 * HALO, cols, 3 * c), BF),
            pltpu.VMEM((2, 2 * HALO, wide, LANES), F32),
            pltpu.VMEM(args[-1].shape, BF),
            pltpu.SemaphoreType.DMA((2,)),
        ],
        cost_estimate=pl.CostEstimate(flops=3_000_000_000, bytes_accessed=6_000_000, transcendentals=2_500_000),
        name="main2",
        compiler_params=pltpu.CompilerParams(vmem_limit_bytes=24 << 20),
    )(*args)


def per_device(
    air_condition_inputs,
    air_embedding_matrix,
    air_blending_matrix,
    exchange_readout_matrix,
    overlay_share_factors,
    marine_condition_inputs,
    water_embedding_matrix,
    drive_lifting_matrix,
    segment_stencil_factors,
    thermal_readout_matrix,
    water_point_indicator,
):
    n_lat, n_lon = lax.axis_size("lat"), lax.axis_size("lon")
    i, j = lax.axis_index("lat"), lax.axis_index("lon")
    bands, width, cells = overlay_share_factors.shape
    fields, rows, cols = marine_condition_inputs.shape
    afields = air_condition_inputs.shape[0]
    share = air_embedding_matrix.shape[1]
    chan = share * n_lon
    near = bands * width
    c = water_embedding_matrix.shape[1]
    where = jnp.stack([i % 2, (i == n_lat - 1).astype(jnp.int32), j % 2]).astype(jnp.int32)

    mine = pl.pallas_call(
        weights_kernel,
        in_specs=[HBM] * 3,
        scratch_shapes=[
            pltpu.VMEM((share, chan), BF),
            pltpu.VMEM((share, afields), BF),
            pltpu.VMEM((exchange_readout_matrix.shape[1], share), BF),
            pltpu.SemaphoreType.DMA((3,)),
        ],
        out_shape=jax.ShapeDtypeStruct((n_lon, share, chan + LANES), BF),
        name="weights",
        compiler_params=pltpu.CompilerParams(vmem_limit_bytes=16 << 20),
    )(*map(in_hbm, (air_blending_matrix.T, air_embedding_matrix.T, exchange_readout_matrix.T)))
    weights = lax.all_to_all(mine, "lon", 0, 0, tiled=True).reshape(chan, chan + LANES)

    marine = jnp.concatenate(
        [
            marine_condition_inputs.reshape(fields, cells),
            water_point_indicator.astype(BF).reshape(1, cells),
            jnp.zeros((MM - fields - 1, cells), BF),
        ],
        0,
    )
    edges = pl.pallas_call(
        edge_kernel,
        in_specs=[SMEM, HBM, VMEM],
        scratch_shapes=[pltpu.VMEM((width, bands, cells), BF), pltpu.SemaphoreType.DMA((5,))],
        out_shape=[jax.ShapeDtypeStruct((near, cells), BF)]
        + [jax.ShapeDtypeStruct((HALO * rows, TILE + LANES), BF)] * 2,
        name="edges",
        compiler_params=pltpu.CompilerParams(vmem_limit_bytes=16 << 20),
    )
    overlay, edge_a, edge_b = edges(where, in_hbm(overlay_share_factors.transpose(1, 0, 2)), marine)
    pairs_b = [(k, ((k - 1) % n_lon ^ 1) + 1) for k in range(n_lon)]
    edge_b = lax.ppermute(edge_b, "lon", [(k, m % n_lon) for k, m in pairs_b])
    edge_a = lax.ppermute(edge_a, "lon", [(k, k ^ 1) for k in range(n_lon)])

    tiles = []
    for d in (-1, 0, 1):
        at = (j + d + n_lon) % n_lon * width
        tile = lax.dynamic_slice_in_dim(air_condition_inputs, at, width, 2)
        tiles.append(jnp.pad(tile.reshape(afields, near), ((0, 0), (0, TILE - near))))
    air = jnp.concatenate(tiles, 1)

    size = HALO * (near + MM) + (TILE + LANES) // LANES * HALO * rows + 3 * 16 * TILE // LANES
    last = cells // (HALO * LANES) - 1
    ends = [
        pl.BlockSpec((d, HALO * LANES), lambda g, k=k: (0, k)) for d in (near, MM) for k in (0, last)
    ]
    whole = [
        pl.BlockSpec((HALO * rows, TILE + LANES), lambda g: (0, 0)),
        pl.BlockSpec((HALO * rows, TILE + LANES), lambda g: (0, 0)),
        pl.BlockSpec((3, 16, TILE), lambda g: (0, 0, 0)),
    ]
    flux = pl.pallas_call(
        own_band_kernel,
        out_shape=jax.ShapeDtypeStruct((3, 16, TILE), BF),
        name="own_band",
        compiler_params=pltpu.CompilerParams(vmem_limit_bytes=16 << 20),
    )(weights, air)
    to_a, to_b = pl.pallas_call(
        pack_kernel,
        grid=(1,),
        in_specs=[SMEM] + ends + whole,
        out_specs=[pl.BlockSpec((size, LANES), lambda g: (0, 0))] * 2,
        out_shape=[jax.ShapeDtypeStruct((size, LANES), BF)] * 2,
        name="pack",
        compiler_params=pltpu.CompilerParams(vmem_limit_bytes=16 << 20),
    )(where, overlay, overlay, marine, marine, edge_a, edge_b, flux)
    pairs_a = [(k, k ^ 1) for k in range(n_lat)]
    pairs_b = []
    for k in range(1, n_lat):
        for m in range(n_lon):
            if k == n_lat - 1:
                other = k * n_lon + n_lon - 1 - m
            else:
                other = (((k - 1) ^ 1) + 1) * n_lon + m
            pairs_b.append((k * n_lon + m, other))
    from_a = lax.ppermute(to_a, "lat", pairs_a)
    from_b = lax.ppermute(to_b, ("lat", "lon"), pairs_b)

    encoder = jnp.concatenate(
        [
            jnp.pad(water_embedding_matrix, ((0, MM - fields), (0, LANES))),
            jnp.pad(drive_lifting_matrix, ((0, 0), (0, LANES))),
            jnp.pad(jnp.broadcast_to(thermal_readout_matrix[None], (8, c)), ((0, 0), (0, LANES))),
        ],
        0,
    )
    r0 = lax.broadcasted_iota(jnp.int32, encoder.shape, 0)
    r1 = lax.broadcasted_iota(jnp.int32, encoder.shape, 1)
    encoder = jnp.where((r0 == fields) & (r1 >= c), jnp.ones((), BF), encoder)
    stencil = in_hbm(segment_stencil_factors.reshape(-1, 9 * c, c))
    sea = water_point_indicator

    mid, s0, m0, s1 = call_main1(
        (where, flux, edge_a, edge_b, overlay, marine, sea, encoder, stencil), rows, cols, c
    )
    return call_main2(
        (where, from_a, from_b, mid, s0, m0, s1, sea, encoder, stencil), rows, cols, c
    )


def solution(mesh):
    return jax.shard_map(
        per_device,
        mesh=mesh,
        in_specs=(
            P(None, "lat", None),
            P(None, "lon"),
            P(None, "lon"),
            P("lon", None),
            P("lat", "lon", None),
            P(None, "lat", "lon"),
            P(),
            P(),
            P(),
            P(),
            P("lat", "lon"),
        ),
        out_specs=P("lat", "lon"),
        check_vma=False,
    )
```

```python
import jax
import jax.numpy as jnp
from jax import lax
from jax.experimental import pallas as pl
from jax.experimental.pallas import tpu as pltpu
from jax.sharding import PartitionSpec as P

BF = jnp.bfloat16
F32 = jnp.float32
LANES = 128
PAD = 8
HALO = 2
MM = 80
TILE = 384
NT = ((1,), (1,))
TN = ((0,), (0,))


def activate(values):
    inner = values * (0.7978845608028654 + 0.035677408136300125 * (values * values))
    half = 0.5 * values
    return half + half * jnp.tanh(inner)


def in_hbm(value):
    return pltpu.with_memory_space_constraint(value, pltpu.HBM)


def dot(a, b, dims=((1,), (0,))):
    return lax.dot_general(a, b, (dims, ((), ())), preferred_element_type=F32)


def one_hot(keep):
    return keep.astype(F32).astype(BF)


def weights_kernel(mix_hbm, emb_hbm, out_hbm, all_ref, mix_ref, emb_ref, out_ref, sems):
    share, chan = mix_ref.shape
    pairs = ((mix_hbm, mix_ref), (emb_hbm, emb_ref), (out_hbm, out_ref))
    copies = [pltpu.make_async_copy(src, dst, sems.at[k]) for k, (src, dst) in enumerate(pairs)]
    for copy in copies:
        copy.start()
    for copy in copies:
        copy.wait()
    for k in range(all_ref.shape[0]):
        all_ref[k, :, :chan] = mix_ref[...]
        all_ref[k, :, chan:] = jnp.zeros((share, LANES), BF)
        all_ref[k, :, chan : chan + emb_ref.shape[1]] = emb_ref[...]
    readout = out_ref[...].astype(F32).T.astype(BF)
    for k in range(all_ref.shape[0]):
        all_ref[k, :, chan + 48 : chan + 56] = readout


def edge_kernel(where_ref, native_hbm, mm_ref, ov_ref, a_ref, b_ref, bulk_ref, native_ref, sems):
    near, cells = ov_ref.shape
    chunks = sems.shape[0]
    size = native_ref.shape[0] // chunks
    copies = []
    for k in range(chunks):
        at = slice(k * size, (k + 1) * size)
        copies.append(pltpu.make_async_copy(native_hbm.at[at], native_ref.at[at], sems.at[k]))
        copies[-1].start()
    n = HALO * cells // LANES
    which = lax.broadcasted_iota(jnp.int32, (2 * n, cells), 0)
    lane = lax.broadcasted_iota(jnp.int32, (2 * n, cells), 1)
    odd = where_ref[2] == 1
    east = (which < n) != odd
    inside = which % n
    target = (inside // HALO) * LANES + inside % HALO + jnp.where(east, LANES - HALO, 0)
    pick = one_hot(lane == target)
    for k, copy in enumerate(copies):
        copy.wait()
        rows = near // chunks
        part = native_ref[k * size : (k + 1) * size].reshape(rows, cells)
        ov_ref[k * rows : (k + 1) * rows, :] = part
    a_ref[...] = jnp.zeros_like(a_ref)
    b_ref[...] = jnp.zeros_like(b_ref)
    got = dot(pick, ov_ref[...], NT).astype(BF)
    a_ref[:, :near] = got[:n]
    b_ref[:, :near] = got[n:]
    got = dot(pick, mm_ref[...], NT).astype(BF)
    a_ref[:, TILE : TILE + MM] = got[:n]
    b_ref[:, TILE : TILE + MM] = got[n:]

    @pl.when(where_ref[0] == 0)
    def _():
        rows_out(bulk_ref, ov_ref, mm_ref, 0)

    @pl.when(where_ref[0] != 0)
    def _():
        rows_out(bulk_ref, ov_ref, mm_ref, cells - HALO * LANES)


def rows_out(dst, ov, mm, first):
    at = 0
    for h in range(HALO):
        lanes = slice(first + h * LANES, first + (h + 1) * LANES)
        for src in (ov, mm):
            dst[at : at + src.shape[0], :] = src[:, lanes]
            at += src.shape[0]


def pack_kernel(where_ref, lo_ref, hi_ref, mlo_ref, mhi_ref, ea_ref, eb_ref, flux_ref, a_ref, b_ref):
    odd = where_ref[2] == 1
    half = ea_ref.shape[0] // 2

    def late(dst, at, top):
        edge = half if top else 0
        for q in range(ea_ref.shape[1] // LANES):
            lanes = slice(q * LANES, (q + 1) * LANES)
            a, b = ea_ref[edge : edge + half, lanes], eb_ref[edge : edge + half, lanes]
            dst[at : at + half, :] = jnp.where(odd, a, b)
            dst[at + half : at + 2 * half, :] = jnp.where(odd, b, a)
            at += 2 * half
        for k in range(3):
            for q in range(TILE // LANES):
                dst[at : at + 16, :] = flux_ref[k, :, q * LANES : (q + 1) * LANES]
                at += 16

    bulk = a_ref.shape[0] - b_ref.shape[0]
    even = where_ref[0] == 0

    @pl.when(even)
    def _():
        rows_out(a_ref, hi_ref, mhi_ref, 0)
        late(a_ref, bulk, True)
        late(b_ref, 0, False)

    @pl.when(jnp.logical_not(even))
    def _():
        rows_out(a_ref, lo_ref, mlo_ref, 0)
        late(a_ref, bulk, False)
        late(b_ref, 0, True)


def own_band_kernel(wts_ref, air_ref, flux):
    chan = wts_ref.shape[0]
    width = NEAR // BANDS
    i0 = lax.broadcasted_iota(jnp.int32, (TILE, TILE), 0)
    i1 = lax.broadcasted_iota(jnp.int32, (TILE, TILE), 1)
    order = one_hot((i0 == (i1 % BANDS) * width + i1 // BANDS) & (i1 < NEAR))
    first = activate(dot(wts_ref[:, chan : chan + 48], air_ref[...])).astype(BF)
    second = activate(dot(wts_ref[:, :chan], first)).astype(BF)
    fluxes = dot(wts_ref[:, chan : chan + LANES], second, TN)[48:56].astype(BF)
    for k in range(3):
        got = dot(fluxes[:, k * TILE : (k + 1) * TILE], order)
        flux[k] = jnp.concatenate([got, jnp.ones_like(got)], 0).astype(BF)


def forced(sums):
    return sums[:8] / jnp.maximum(sums[8:], 0.25)


def fill(z, lanes, fields, sums):
    z[:MM, lanes] = fields
    z[MM:, lanes] = jnp.concatenate([forced(sums), jnp.zeros_like(sums[:8])], 0).astype(BF)


def edge_cells(table, flu, wenc_ref):
    c = wenc_ref.shape[1] - LANES
    weighted, coverage = dot(table[:, :TILE], flu[:8], NT), dot(table[:, :TILE], flu[8:], NT)
    forcing = (weighted / jnp.maximum(coverage, 0.25)).astype(BF)
    enc = dot(table[:, TILE : TILE + MM], wenc_ref[:MM])
    state = enc[:, :c] + dot(forcing, wenc_ref[MM : MM + 8, :c])
    m = enc[:, c:]
    state = activate(state) * jnp.concatenate([m, m], 1)
    return jnp.concatenate([state.astype(BF), m.astype(BF)], 1)


def encoded_row(z, lanes, wenc_ref, west, east):
    c = wenc_ref.shape[1] - LANES
    enc = dot(z[:, lanes], wenc_ref[...], TN)
    m = enc[:, c:]
    state = (activate(enc[:, :c]) * jnp.concatenate([m, m], 1)).astype(BF).astype(F32)
    return (
        jnp.concatenate([west[:, :c], state, east[:, :c]], 0),
        jnp.concatenate([west[:, c:], m, east[:, c:]], 0),
    )


def three_shifts(dst, row):
    c = row.shape[1]
    dst[:, c : 2 * c] = row.astype(BF)
    dst[:, :c] = pltpu.roll(row, 1, 0).astype(BF)
    dst[:, 2 * c :] = pltpu.roll(row, row.shape[0] - 1, 0).astype(BF)


def inner_shifts(dst, row):
    c = row.shape[1]
    for k in range(3):
        moved = pltpu.roll(row, row.shape[0] - (PAD - 1 + k), 0)[:LANES]
        dst[:, k * c : (k + 1) * c] = moved.astype(BF)


def taps(window, kernel):
    conv = None
    for a in range(3):
        lhs = window(a)
        term = dot(lhs, kernel[a * lhs.shape[1] : (a + 1) * lhs.shape[1], :])
        conv = term if conv is None else conv + term
    return conv


def section(state, m, conv):
    return jnp.concatenate([m, m], 1) * (state.astype(F32) + activate(conv))


def main1_kernel(
    where_ref, flux, ea_ref, eb_ref, ov_ref, mm_ref, sea_ref, wenc_ref, kw_hbm,
    mid_ref, shifted, mask, shifted2,
    z, side, kw_ref, sems,
):
    near, cells = ov_ref.shape
    rows = cells // LANES
    c = kw_ref.shape[2]
    n = HALO * rows
    wide = LANES + 2 * PAD
    odd = where_ref[2] == 1
    copies = [pltpu.make_async_copy(kw_hbm.at[k], kw_ref.at[k], sems.at[k]) for k in range(2)]
    for copy in copies:
        copy.start()

    fill(z, slice(0, cells), mm_ref[...], dot(flux[1, :, :near], ov_ref[...]))

    for s in range(2):
        a, b = ea_ref[...], eb_ref[...]
        table = jnp.where(odd, a, b) if s == 0 else jnp.where(odd, b, a)
        table = edge_cells(table, flux[2 * s], wenc_ref)
        at = lax.broadcasted_iota(jnp.int32, (rows * PAD, n), 0)
        lane = lax.broadcasted_iota(jnp.int32, (rows * PAD, n), 1)
        dx = at % PAD - (PAD - HALO if s == 0 else 0)
        keep = (lane == at // PAD * HALO + dx) & (dx >= 0) & (dx < HALO)
        side[s] = dot(one_hot(keep), table)

    def own_row(y):
        lanes = slice(y * LANES, (y + 1) * LANES)
        at = slice(y * PAD, (y + 1) * PAD)
        row, m = encoded_row(z, lanes, wenc_ref, side[0, at, :], side[1, at, :])
        mask[y] = m
        three_shifts(shifted.at[y], row)

    for y in range(rows):
        own_row(y)
    step = 7

    def first(g, _):
        y = g * step + 1
        conv = taps(lambda a: shifted[pl.ds(y - 1 + a, step)].reshape(step * wide, 3 * c), kw_ref.at[0])
        state = shifted[pl.ds(y, step), :, c : 2 * c].reshape(step * wide, c)
        state = section(state, mask[pl.ds(y, step)].reshape(step * wide, LANES), conv)
        state = state.astype(BF).astype(F32)
        for q in range(step):
            inner_shifts(shifted2.at[y + q], state[q * wide : (q + 1) * wide])
        return 0

    copies[0].wait()
    lax.fori_loop(0, (rows - 2) // step, first, 0)
    step2 = 12

    def second(g, _):
        y = g * step2 + 2
        conv = taps(
            lambda a: shifted2[pl.ds(y - 1 + a, step2)].reshape(step2 * LANES, 3 * c), kw_ref.at[1]
        )
        state = shifted2[pl.ds(y, step2), :, c : 2 * c].reshape(step2 * LANES, c)
        m = mask[pl.ds(y, step2), PAD : PAD + LANES, :].reshape(step2 * LANES, LANES)
        got = dot(wenc_ref[MM + 8 :, :c], section(state, m, conv).astype(BF), NT)
        for q in range(step2):
            row = got[:1, q * LANES : (q + 1) * LANES]
            mid_ref[pl.ds(y + q, 1), :] = row * sea_ref[pl.ds(y + q, 1), :].astype(F32)
        return 0

    copies[1].wait()
    lax.fori_loop(0, (rows - 4) // step2, second, 0)


def main2_kernel(
    where_ref, pa_ref, bulk_ref, pb_ref, mid_ref, s0_ref, m0_ref, s1_ref, sea_ref, wenc_ref, kw_hbm,
    out_ref,
    flux, z, side, shifted, shifted2, mask, kw_ref, sems,
):
    rows = out_ref.shape[0]
    near = NEAR
    c = kw_ref.shape[2]
    half = HALO * rows // 2
    wide = LANES + 2 * PAD
    even = where_ref[0] == 0
    north = where_ref[1] == 1
    at_edge = HALO * (near + MM)
    at_flux = at_edge + (TILE + LANES) // LANES * 2 * half
    copies = [pltpu.make_async_copy(kw_hbm.at[k], kw_ref.at[k], sems.at[k]) for k in range(2)]
    for copy in copies:
        copy.start()

    def halo(which, lo, size):
        a = pa_ref[lo : lo + size, :]
        b = bulk_ref[lo : lo + size, :] if lo < at_edge else pb_ref[lo - at_edge : lo - at_edge + size, :]
        return jnp.where(even, b, a) if which == 0 else jnp.where(even, a, b)

    for which in range(2):
        for k in range(3):
            for q in range(TILE // LANES):
                at = at_flux + (k * (TILE // LANES) + q) * 16
                flux[3 * which + k, :, q * LANES : (q + 1) * LANES] = halo(which, at, 16)
    for which in range(2):
        for h in range(HALO):
            sums = dot(flux[3 * which + 1, :, :near], halo(which, h * (near + MM), near))
            at = (which * HALO + h) * LANES
            fill(z, slice(at, at + LANES), halo(which, h * (near + MM) + near, MM), sums)
    for s in range(2):
        parts = []
        for which in range(2):
            table = [
                halo(which, at_edge + q * 2 * half + s * half, half) for q in range((TILE + LANES) // LANES)
            ]
            parts.append(edge_cells(jnp.concatenate(table, 1), flux[3 * which + 2 * s], wenc_ref))
        table = jnp.concatenate(parts, 0)
        at = lax.broadcasted_iota(jnp.int32, (2 * HALO * PAD, 2 * half), 0)
        lane = lax.broadcasted_iota(jnp.int32, (2 * HALO * PAD, 2 * half), 1)
        row, dx = at // PAD, at % PAD - (PAD - HALO if s == 0 else 0)
        last = half - HALO * HALO
        source = jnp.where(
            row < HALO, last + row * HALO, half + (row - HALO) * HALO + jnp.where(north, last, 0)
        )
        keep = (lane == source + dx) & (dx >= 0) & (dx < HALO)
        side[s] = dot(one_hot(keep), table)

    new = []
    for q in range(2 * HALO):
        at = slice(q * PAD, (q + 1) * PAD)
        lanes = slice(q * LANES, (q + 1) * LANES)
        new.append(encoded_row(z, lanes, wenc_ref, side[0, at, :], side[1, at, :]))

    def put(strip, y, row, m):
        mask[strip, y] = m
        three_shifts(shifted.at[strip, y], row)

    for h in range(HALO):
        put(0, h, *new[h])
        shifted[0, HALO + h] = s0_ref[h]
        mask[0, HALO + h] = m0_ref[h]
        shifted[1, h] = s0_ref[rows - HALO + h]
        mask[1, h] = m0_ref[rows - HALO + h]
        shifted2[0, HALO + h] = s1_ref[1 + h]
        shifted2[1, h] = s1_ref[rows - 1 - HALO + h]

    @pl.when(jnp.logical_not(north))
    def _():
        for h in range(HALO):
            put(1, HALO + h, *new[HALO + h])

    @pl.when(north)
    def _():
        i0 = lax.broadcasted_iota(jnp.int32, (wide, wide), 0)
        i1 = lax.broadcasted_iota(jnp.int32, (wide, wide), 1)
        turn = one_hot(i0 + i1 == wide - 1)
        for h in range(HALO):
            row, m = new[2 * HALO - 1 - h]
            put(1, HALO + h, dot(turn, row.astype(BF)), dot(turn, m.astype(BF)))

    copies[0].wait()
    size = 2 * HALO * wide
    conv = taps(lambda a: shifted[:, a : a + HALO].reshape(size, 3 * c), kw_ref.at[0])
    state = shifted[:, 1 : 1 + HALO, :, c : 2 * c].reshape(size, c)
    state = section(state, mask[:, 1 : 1 + HALO].reshape(size, LANES), conv).astype(BF).astype(F32)
    for q in range(2 * HALO):
        strip, y = q // HALO, q % HALO
        inner_shifts(shifted2.at[strip, HALO * strip + y], state[q * wide : (q + 1) * wide])

    @pl.when(north)
    def _():
        conv = None
        for a in range(3):
            for b in range(3):
                lhs = shifted[1, 3 - a, :, (2 - b) * c : (3 - b) * c]
                at = (3 * a + b) * c
                term = dot(lhs, kw_ref[0, at : at + c, :])
                conv = term if conv is None else conv + term
        state = section(shifted[1, 2, :, c : 2 * c], mask[1, 2], conv).astype(BF).astype(F32)
        inner_shifts(shifted2.at[1, 3], state)

    copies[1].wait()
    size = 2 * HALO * LANES
    conv = taps(lambda a: shifted2[:, a : a + HALO].reshape(size, 3 * c), kw_ref.at[1])
    state = shifted2[:, 1 : 1 + HALO, :, c : 2 * c].reshape(size, c)
    inner = slice(PAD, PAD + LANES)
    m = jnp.concatenate([mask[0, HALO:, inner, :], mask[1, :HALO, inner, :]], 0).reshape(size, LANES)
    got = dot(wenc_ref[MM + 8 :, :c], section(state, m, conv).astype(BF), NT)
    out_ref[...] = mid_ref[...]
    for q, y in enumerate((0, 1, rows - 2, rows - 1)):
        row = got[:1, q * LANES : (q + 1) * LANES]
        out_ref[y : y + 1, :] = row * sea_ref[y : y + 1, :].astype(F32)


BANDS = 4
NEAR = 360
VMEM = pl.BlockSpec(memory_space=pltpu.VMEM)
SMEM = pl.BlockSpec(memory_space=pltpu.SMEM)
HBM = pl.BlockSpec(memory_space=pltpu.HBM)


def call_main1(args, rows, cols, c):
    wide = cols + 2 * PAD
    return pl.pallas_call(
        main1_kernel,
        in_specs=[SMEM] + [VMEM] * 7 + [HBM],
        out_shape=[
            jax.ShapeDtypeStruct((rows, cols), F32),
            jax.ShapeDtypeStruct((rows, wide, 3 * c), BF),
            jax.ShapeDtypeStruct((rows, wide, LANES), F32),
            jax.ShapeDtypeStruct((rows, cols, 3 * c), BF),
        ],
        scratch_shapes=[
            pltpu.VMEM((MM + 16, rows * cols), BF),
            pltpu.VMEM((2, rows * PAD, c + LANES), F32),
            pltpu.VMEM(args[-1].shape, BF),
            pltpu.SemaphoreType.DMA((2,)),
        ],
        cost_estimate=pl.CostEstimate(flops=6_000_000_000, bytes_accessed=8_000_000, transcendentals=2_000_000),
        name="main1",
        compiler_params=pltpu.CompilerParams(vmem_limit_bytes=30 << 20),
    )(*args)


def call_main2(args, rows, cols, c):
    wide = cols + 2 * PAD
    return pl.pallas_call(
        main2_kernel,
        in_specs=[SMEM] + [VMEM] * 9 + [HBM],
        out_shape=jax.ShapeDtypeStruct((rows, cols), F32),
        scratch_shapes=[
            pltpu.VMEM((6, 16, TILE), BF),
            pltpu.VMEM((MM + 16, 2 * HALO * cols), BF),
            pltpu.VMEM((2, 2 * HALO * PAD, c + LANES), F32),
            pltpu.VMEM((2, 2 * HALO, wide, 3 * c), BF),
            pltpu.VMEM((2, 2 * HALO, cols, 3 * c), BF),
            pltpu.VMEM((2, 2 * HALO, wide, LANES), F32),
            pltpu.VMEM(args[-1].shape, BF),
            pltpu.SemaphoreType.DMA((2,)),
        ],
        cost_estimate=pl.CostEstimate(flops=3_000_000_000, bytes_accessed=6_000_000, transcendentals=2_500_000),
        name="main2",
        compiler_params=pltpu.CompilerParams(vmem_limit_bytes=24 << 20),
    )(*args)


def per_device(
    air_condition_inputs,
    air_embedding_matrix,
    air_blending_matrix,
    exchange_readout_matrix,
    overlay_share_factors,
    marine_condition_inputs,
    water_embedding_matrix,
    drive_lifting_matrix,
    segment_stencil_factors,
    thermal_readout_matrix,
    water_point_indicator,
):
    n_lat, n_lon = lax.axis_size("lat"), lax.axis_size("lon")
    i, j = lax.axis_index("lat"), lax.axis_index("lon")
    bands, width, cells = overlay_share_factors.shape
    fields, rows, cols = marine_condition_inputs.shape
    afields = air_condition_inputs.shape[0]
    share = air_embedding_matrix.shape[1]
    chan = share * n_lon
    near = bands * width
    c = water_embedding_matrix.shape[1]
    where = jnp.stack([i % 2, (i == n_lat - 1).astype(jnp.int32), j % 2]).astype(jnp.int32)

    mine = pl.pallas_call(
        weights_kernel,
        in_specs=[HBM] * 3,
        scratch_shapes=[
            pltpu.VMEM((share, chan), BF),
            pltpu.VMEM((share, afields), BF),
            pltpu.VMEM((exchange_readout_matrix.shape[1], share), BF),
            pltpu.SemaphoreType.DMA((3,)),
        ],
        out_shape=jax.ShapeDtypeStruct((n_lon, share, chan + LANES), BF),
        name="weights",
        compiler_params=pltpu.CompilerParams(vmem_limit_bytes=16 << 20),
    )(*map(in_hbm, (air_blending_matrix.T, air_embedding_matrix.T, exchange_readout_matrix.T)))
    weights = lax.all_to_all(mine, "lon", 0, 0, tiled=True).reshape(chan, chan + LANES)

    marine = jnp.concatenate(
        [
            marine_condition_inputs.reshape(fields, cells),
            water_point_indicator.astype(BF).reshape(1, cells),
            jnp.zeros((MM - fields - 1, cells), BF),
        ],
        0,
    )
    bulk = HALO * (near + MM)
    edges = pl.pallas_call(
        edge_kernel,
        in_specs=[SMEM, HBM, VMEM],
        scratch_shapes=[pltpu.VMEM((width, bands, cells), BF), pltpu.SemaphoreType.DMA((5,))],
        out_shape=[jax.ShapeDtypeStruct((near, cells), BF)]
        + [jax.ShapeDtypeStruct((HALO * rows, TILE + LANES), BF)] * 2
        + [jax.ShapeDtypeStruct((bulk, LANES), BF)],
        name="edges",
        compiler_params=pltpu.CompilerParams(vmem_limit_bytes=16 << 20),
    )
    overlay, edge_a, edge_b, to_bulk = edges(where, in_hbm(overlay_share_factors.transpose(1, 0, 2)), marine)
    pairs_b = [(k, ((k - 1) % n_lon ^ 1) + 1) for k in range(n_lon)]
    edge_b = lax.ppermute(edge_b, "lon", [(k, m % n_lon) for k, m in pairs_b])
    edge_a = lax.ppermute(edge_a, "lon", [(k, k ^ 1) for k in range(n_lon)])

    pairs_a = [(k, k ^ 1) for k in range(n_lat)]
    across = []
    for k in range(1, n_lat):
        for m in range(n_lon):
            if k == n_lat - 1:
                other = k * n_lon + n_lon - 1 - m
            else:
                other = (((k - 1) ^ 1) + 1) * n_lon + m
            across.append((k * n_lon + m, other))
    from_bulk = lax.ppermute(to_bulk, ("lat", "lon"), across)

    tiles = []
    for d in (-1, 0, 1):
        at = (j + d + n_lon) % n_lon * width
        tile = lax.dynamic_slice_in_dim(air_condition_inputs, at, width, 2)
        tiles.append(jnp.pad(tile.reshape(afields, near), ((0, 0), (0, TILE - near))))
    air = jnp.concatenate(tiles, 1)

    late = (TILE + LANES) // LANES * HALO * rows + 3 * 16 * TILE // LANES
    last = cells // (HALO * LANES) - 1
    ends = [
        pl.BlockSpec((d, HALO * LANES), lambda g, k=k: (0, k)) for d in (near, MM) for k in (0, last)
    ]
    whole = [
        pl.BlockSpec((HALO * rows, TILE + LANES), lambda g: (0, 0)),
        pl.BlockSpec((HALO * rows, TILE + LANES), lambda g: (0, 0)),
        pl.BlockSpec((3, 16, TILE), lambda g: (0, 0, 0)),
    ]
    flux = pl.pallas_call(
        own_band_kernel,
        out_shape=jax.ShapeDtypeStruct((3, 16, TILE), BF),
        name="own_band",
        compiler_params=pltpu.CompilerParams(vmem_limit_bytes=16 << 20),
    )(weights, air)
    to_a, to_b = pl.pallas_call(
        pack_kernel,
        grid=(1,),
        in_specs=[SMEM] + ends + whole,
        out_specs=[pl.BlockSpec((d, LANES), lambda g: (0, 0)) for d in (bulk + late, late)],
        out_shape=[jax.ShapeDtypeStruct((d, LANES), BF) for d in (bulk + late, late)],
        name="pack",
        compiler_params=pltpu.CompilerParams(vmem_limit_bytes=16 << 20),
    )(where, overlay, overlay, marine, marine, edge_a, edge_b, flux)
    from_a = lax.ppermute(to_a, "lat", pairs_a)
    from_b = lax.ppermute(to_b, ("lat", "lon"), across)

    encoder = jnp.concatenate(
        [
            jnp.pad(water_embedding_matrix, ((0, MM - fields), (0, LANES))),
            jnp.pad(drive_lifting_matrix, ((0, 0), (0, LANES))),
            jnp.pad(jnp.broadcast_to(thermal_readout_matrix[None], (8, c)), ((0, 0), (0, LANES))),
        ],
        0,
    )
    r0 = lax.broadcasted_iota(jnp.int32, encoder.shape, 0)
    r1 = lax.broadcasted_iota(jnp.int32, encoder.shape, 1)
    encoder = jnp.where((r0 == fields) & (r1 >= c), jnp.ones((), BF), encoder)
    stencil = in_hbm(segment_stencil_factors.reshape(-1, 9 * c, c))
    sea = water_point_indicator

    mid, s0, m0, s1 = call_main1(
        (where, flux, edge_a, edge_b, overlay, marine, sea, encoder, stencil), rows, cols, c
    )
    return call_main2(
        (where, from_a, from_bulk, from_b, mid, s0, m0, s1, sea, encoder, stencil), rows, cols, c
    )


def solution(mesh):
    return jax.shard_map(
        per_device,
        mesh=mesh,
        in_specs=(
            P(None, "lat", None),
            P(None, "lon"),
            P(None, "lon"),
            P("lon", None),
            P("lat", "lon", None),
            P(None, "lat", "lon"),
            P(),
            P(),
            P(),
            P(),
            P("lat", "lon"),
        ),
        out_specs=P("lat", "lon"),
        check_vma=False,
    )
```
